32 devices in a mesh: blk: 8 (over z, x), aux: 4 (over y, core).
Axes of the slice: x: 2, y: 2, z: 4, core: 2. Of those that a mesh axis runs over, the one named last changes fastest.
Arguments:
- half_ints: bfloat16 [32, 1536, 384], P('blk', 'aux'), may hold values from -0.625 to 0.625
- metric_inv: bfloat16 [1536, 1536], P('aux'), may hold values from -1 to 2, as said below
- occ_energy: float32 [32], replicated, may hold values from -2 to -0.3
- vir_energy: float32 [384], replicated, may hold values from 0.3 to 3
Outputs:
- gamma: bfloat16 [32, 1536, 384], P('blk', 'aux')
The draws below stay inside these ranges and needn't reach their ends.
Inputs may be any that keep to these rules, and one draw needn't show every extreme that they name: metric_inv is lower triangular (zero where Q > P) with a positive diagonal.
All inputs are finite; a program needn't handle non-finite values.
Results may differ from the reference program's by a relative error of at most 0.0058.
Values may be sent and summed in bfloat16 or wider, within the bound.
A program may use at most 64 MiB of HBM per device.

```python
import math
import jax
import jax.numpy as jnp
from jax import lax

VIR = 384
NAUX = 1536
OCC_SUB = 1
CYCLE = 4
NOCC = 32
N_AUX = 4


def draw_metric_inv(key, part):
    first_key, second_key = jax.random.split(key)
    row_index = lax.broadcasted_iota(jnp.int32, (NAUX, NAUX), 0)
    col_index = lax.broadcasted_iota(jnp.int32, (NAUX, NAUX), 1)
    lower_part = jnp.clip(jax.random.normal(first_key, (NAUX, NAUX), jnp.float32), -4.0, 4.0) * 0.8
    lower_part = lower_part * NAUX ** (-0.5)
    diagonal = jnp.exp(jax.random.uniform(second_key, (NAUX,), jnp.float32, math.log(0.5), math.log(2.0)))
    lower_part = jnp.where(row_index > col_index, lower_part, 0.0)
    return (lower_part + jnp.where(row_index == col_index, diagonal[None, :], 0.0)).astype(jnp.bfloat16)


def level_of(own_key, shape, shards, low, high):
    level = 1.0
    for dim, shards_of in shards:
        draws = jax.random.uniform(jax.random.fold_in(jax.random.fold_in(own_key, 6), dim), (shards_of,), jnp.float32, low / len(shards), high / len(shards))
        level = level * jnp.repeat(jnp.exp(draws), shape[dim] // shards_of).reshape((-1,) + (1,) * (len(shape) - 1 - dim))
    return level


def normal_values(rng, extent, width, bound, cuts=(), held_as=jnp.bfloat16):
    values = jax.random.normal(rng, extent, jnp.float32) * width
    if len(cuts) > 0:
        values = level_of(rng, extent, cuts, -0.22, 0.18) * values
    return jnp.clip(values, min=-bound, max=bound).astype(held_as)


def setup_inputs(seed: int = 0) -> dict:
    key_list = jax.random.split(jax.random.key(seed), 5)
    return {
        "half_ints": normal_values(key_list[0], (NOCC, NAUX, VIR), 0.1, 0.625, ((0, 8), (1, 4))),
        "metric_inv": draw_metric_inv(jax.random.fold_in(key_list[4], 71), 0),
        "occ_energy": jnp.clip(jax.random.uniform(key_list[2], (NOCC,), jnp.float32, -2.0, -0.3), -2.0, -0.3),
        "vir_energy": jnp.clip(jax.random.uniform(key_list[3], (VIR,), jnp.float32, 0.3, 3.0), 0.3, 3.0),
    }


def reference(half_ints, metric_inv, occ_energy, vir_energy):
    unit_count = NOCC // OCC_SUB
    metric_f32 = metric_inv.astype(jnp.float32)

    def fit_unit(occ_block):
        return jnp.einsum("pq,upa->uqa", metric_f32, occ_block.astype(jnp.float32)).astype(jnp.bfloat16)

    fitted = lax.map(fit_unit, half_ints.reshape(unit_count, OCC_SUB, NAUX, VIR))
    energies = occ_energy.astype(jnp.float32).reshape(unit_count, OCC_SUB)
    virtuals = vir_energy.astype(jnp.float32)

    def density_unit(unit_index):
        own_block = fitted[unit_index].astype(jnp.float32)
        own_energy = energies[unit_index]
        density_acc = jnp.zeros((OCC_SUB, NAUX, VIR), jnp.float32)
        for cycle_step in range(CYCLE):
            partner_index = ((unit_index - cycle_step * N_AUX) % unit_count).astype(jnp.int32)
            partner = fitted[partner_index].astype(jnp.float32)
            partner_energy = energies[partner_index]
            pair_ints = jnp.einsum("uqa,vqb->uvab", own_block, partner)
            energy_gap = (own_energy[:, None, None, None] + partner_energy[None, :, None, None]
                          - virtuals[None, None, :, None] - virtuals[None, None, None, :])
            amplitude = ((2.0 * pair_ints - jnp.swapaxes(pair_ints, 2, 3)) / energy_gap).astype(jnp.bfloat16)
            density_acc = density_acc + jnp.einsum("uvab,vqb->uqa", amplitude.astype(jnp.float32), partner)
        density_fit = density_acc.astype(jnp.bfloat16)
        return jnp.einsum("pq,uqa->upa", metric_f32, density_fit.astype(jnp.float32)).astype(jnp.bfloat16)

    gamma = lax.map(density_unit, jnp.arange(unit_count, dtype=jnp.int32))
    return gamma.reshape(NOCC, NAUX, VIR)
```

```python
import functools

import jax
import jax.numpy as jnp
from jax import lax
from jax.experimental import pallas as pl
from jax.experimental.pallas import tpu as pltpu
from jax.sharding import PartitionSpec as P

CYCLE = 4
MESH = pl.DeviceIdType.MESH


def kernel(
    blocks, groups, tile,
    ints_ref, metric_ref, occ_ref, vir_ref,
    out_ref,
    ints, metric, metric_t, fits, fit_t, gap, pair_sum, dens, dens_b, gam,
    h_send, h_recv, d_send, z_send, w_send, ring_recv, f_send, f_recv,
    m1_send, m1_recv, m2_send, m2_recv, m3_send, m3_recv, own_sem, g_send, g_recv,
):
    shard = ints_ref.shape[1]
    half = shard // 2
    parts = 4 if half % 64 == 0 else 1
    part = half // parts
    naux = metric_ref.shape[1]
    vir = ints_ref.shape[2]
    tiles = naux // tile
    pairs = groups // 2
    b, g = lax.axis_index("blk"), lax.axis_index("aux")
    x, core, h = b % 2, g % 2, g // 2
    plane, mate, ahead = b - x, g + 1 - 2 * core, (b + 2) % blocks
    across = b + 1 - 2 * x
    own_b, own_c = plane + core, g - core + x
    f32 = jnp.float32

    def rows(p):
        return pl.ds(pl.multiple_of(p * shard, shard), shard)

    def slab(p, which, n):
        return pl.ds(pl.multiple_of(p * shard + which * half + n * part, part), part)

    def span(q):
        return pl.ds(pl.multiple_of(q * tile, tile), tile)

    def width(hv):
        return min(naux, -(-2 * shard * (hv + 1) // tile) * tile)

    def remote(src, dst, send, recv, device):
        return pltpu.make_async_remote_copy(
            src_ref=src, dst_ref=dst, send_sem=send, recv_sem=recv,
            device_id=device, device_id_type=MESH,
        )

    def landed(dst, recv):
        pltpu.make_async_copy(dst, dst, recv).wait()

    barrier = pltpu.get_barrier_semaphore()
    for xx in range(2):
        for gg in range(groups):
            @pl.when((plane + xx != b) | (gg != g))
            def _():
                pl.semaphore_signal(barrier, inc=1, device_id=(plane + xx, gg), device_id_type=MESH)
    for bb in (ahead, (b + blocks - 2) % blocks):
        for gg in (g, mate):
            pl.semaphore_signal(barrier, inc=1, device_id=(bb, gg), device_id_type=MESH)
    pl.semaphore_wait(barrier, 2 * groups + 3)

    def ints_copy(c):
        return remote(
            ints_ref.at[c], ints.at[0, rows(g)], h_send.at[c], h_recv.at[g],
            (plane + c % 2, c - c % 2 + x),
        )

    def to_self(c):
        return (core == x) & (c == own_c)

    order = [(2 * ((h + r) % pairs) + par) for r in range(pairs) for par in range(2)]
    tail_first = [groups - 2] + [p for p in range(groups - 1, -1, -1) if p != groups - 2]

    def d_copy():
        return remote(
            ints_ref.at[own_c], ints.at[2, rows(g)], d_send, ring_recv.at[2, g], (ahead, own_c)
        )

    d_copy().start()
    for c in order:
        @pl.when(jnp.logical_not(to_self(c)))
        def _():
            ints_copy(c).start()

        @pl.when(to_self(c))
        def _():
            pltpu.make_async_copy(ints_ref.at[c], ints.at[0, rows(g)], h_recv.at[g]).start()

    own_metric = pltpu.make_async_copy(metric_ref, metric.at[rows(g)], own_sem)
    own_metric.start()

    def m1_copy(hv, r, n):
        return remote(
            metric_ref.at[slab(0, x, n), pl.ds(0, width(hv))],
            metric.at[slab(g, x, n), pl.ds(0, width(hv))],
            m1_send.at[r, n], m1_recv.at[hv, n],
            (b, 2 * ((h + r) % pairs) + core),
        )

    def m3_own(hv):
        return remote(
            metric_ref.at[:, pl.ds(0, width(hv))], metric.at[rows(g), pl.ds(0, width(hv))],
            m3_send.at[hv], m3_recv.at[hv], (b, mate),
        )

    def m2_copy(hv, n):
        piece = metric.at[slab(2 * hv + core, x, n), pl.ds(0, width(hv))]
        return remote(piece, piece, m2_send.at[hv, n], m2_recv.at[hv, n], (across, g))

    def m3_copy(hv):
        piece = metric.at[rows(2 * hv + core), pl.ds(0, width(hv))]
        return remote(piece, piece, m3_send.at[hv], m3_recv.at[hv], (b, mate))

    for hv in range(pairs):
        @pl.when(h == hv)
        def _():
            for r in range(1, pairs):
                for n in range(parts):
                    m1_copy(hv, r, n).start()
            m3_own(hv).start()

    def z_copy(p):
        return remote(ints.at[0, rows(p)], ints.at[2, rows(p)], z_send.at[p], ring_recv.at[2, p], (ahead, g))

    def w_copy(p):
        return remote(ints.at[2, rows(p)], ints.at[3, rows(p)], w_send.at[p], ring_recv.at[3, p], (ahead, mate))

    def sent_up(p):
        return jnp.logical_not((core == x) & (p // 2 == h))

    def f_copy(src, dst):
        return remote(fits.at[src], fits.at[dst], f_send.at[dst // 2], f_recv.at[dst // 2], (b, mate))

    levels = jnp.broadcast_to(vir_ref[...], (vir, vir))
    gap[...] = levels + levels.T

    for p in order:
        landed(ints.at[0, rows(p)], h_recv.at[p])

        @pl.when(sent_up(p))
        def _():
            z_copy(p).start()

    for hv in range(pairs):
        @pl.when(h != hv)
        def _():
            for n in range(parts):
                landed(metric.at[slab(2 * hv + core, x, n), pl.ds(0, width(hv))], m1_recv.at[hv, n])
                m2_copy(hv, n).start()
    for hv in range(pairs):
        @pl.when(h != hv)
        def _():
            for n in range(parts):
                landed(metric.at[slab(2 * hv + core, 1 - x, n), pl.ds(0, width(hv))], m2_recv.at[hv, n])
            m3_copy(hv).start()

    for p in tail_first:
        landed(ints.at[2, rows(p)], ring_recv.at[2, p])

        @pl.when(core == 1)
        def _():
            w_copy(p).start()

    own_metric.wait()
    for hv in range(pairs):
        landed(metric.at[rows(2 * hv + 1 - core), pl.ds(0, width(hv))], m3_recv.at[hv])

    @pl.loop(0, tiles)
    def _(p):
        @pl.loop(0, p + 1)
        def _(q):
            metric_t[span(q), span(p)] = metric[span(p), span(q)].T

    own_energy = occ_ref[own_b * groups + own_c]

    def fit_tile(role, q):
        low = q * tile
        fits[role, low:low + tile, :] = jnp.dot(
            metric_t[low:low + tile, low:], ints[role, low:, :], preferred_element_type=f32,
        ).astype(fits.dtype)

    def amplitude_of(pair, role):
        energy = own_energy + occ_ref[(own_b + blocks - role) % blocks * groups + own_c]
        return ((2.0 * pair.T - pair) / (energy - gap[...])).astype(fits.dtype)

    for role in (0, 2):
        for q in range(tiles):
            fit_tile(role, q)

        @pl.when(core == 0)
        def _():
            f_copy(role, role + 1).start()

        if role == 2:
            @pl.when(core == 1)
            def _():
                f_copy(2, 1).start()

    @pl.loop(0, tiles)
    def _(q):
        fit_t[:, span(q)] = fits[0, span(q), :].T

    @pl.loop(0, CYCLE - 1)
    def _(k):
        role = 2 * k - 3 * (k // 2)

        @pl.when(k == 2)
        def _():
            landed(fits.at[1], f_recv.at[0])

        pair = jnp.dot(fit_t[...], fits[role], preferred_element_type=f32)
        amplitude_t = amplitude_of(pair, role)

        @pl.when(k == 0)
        def _():
            dens[...] = jnp.dot(fits[role], amplitude_t, preferred_element_type=f32)

        @pl.when(k > 0)
        def _():
            dens[...] += jnp.dot(fits[role], amplitude_t, preferred_element_type=f32)

    @pl.when(core == 1)
    def _():
        landed(fits.at[3], f_recv.at[1])
        pair_sum[...] = jnp.dot(fit_t[...], fits[3], preferred_element_type=f32)

    @pl.when(core == 0)
    def _():
        for q in reversed(range(tiles)):
            low = q * tile
            for p in reversed(range(low // shard, (low + tile) // shard)):
                landed(ints.at[3, rows(p)], ring_recv.at[3, p])
            fit_tile(3, q)
            part_sum = jnp.dot(
                fit_t[:, low:low + tile], fits[3, low:low + tile, :], preferred_element_type=f32
            )
            if q == tiles - 1:
                pair_sum[...] = part_sum
            else:
                pair_sum[...] += part_sum

    amplitude_t = amplitude_of(pair_sum[...], 3)

    def g_copy(p):
        return remote(gam.at[rows(p)], out_ref.at[own_c], g_send.at[p], g_recv.at[own_c], (own_b, p))

    def g_self(p):
        return (core == x) & (g == p)

    for t in range(tiles):
        low = t * tile
        total = dens[low:low + tile, :] + jnp.dot(
            fits[3, low:low + tile, :], amplitude_t, preferred_element_type=f32
        )
        dens_b[low:low + tile, :] = total.astype(dens_b.dtype)
        gam[low:low + tile, :] = jnp.dot(
            metric[low:low + tile, :low + tile], dens_b[:low + tile, :],
            preferred_element_type=f32,
        ).astype(gam.dtype)
        for p in range(low // shard, (low + tile) // shard):
            @pl.when(jnp.logical_not(g_self(p)))
            def _():
                g_copy(p).start()

            @pl.when(g_self(p))
            def _():
                pltpu.make_async_copy(gam.at[rows(p)], out_ref.at[own_c], g_recv.at[own_c]).start()

    d_copy().wait_send()
    for c in range(groups):
        @pl.when(jnp.logical_not(to_self(c)))
        def _():
            ints_copy(c).wait_send()

        @pl.when(sent_up(c))
        def _():
            z_copy(c).wait_send()

        @pl.when(core == 1)
        def _():
            w_copy(c).wait_send()

        @pl.when(jnp.logical_not(g_self(c)))
        def _():
            g_copy(c).wait_send()

    @pl.when(core == 0)
    def _():
        f_copy(0, 1).wait_send()
        f_copy(2, 3).wait_send()

    @pl.when(core == 1)
    def _():
        f_copy(2, 1).wait_send()

    for hv in range(pairs):
        @pl.when(h == hv)
        def _():
            for r in range(1, pairs):
                for n in range(parts):
                    m1_copy(hv, r, n).wait_send()
            m3_own(hv).wait_send()

        @pl.when(h != hv)
        def _():
            for n in range(parts):
                m2_copy(hv, n).wait_send()
            m3_copy(hv).wait_send()
    for c in range(groups):
        landed(out_ref.at[c], g_recv.at[c])


def local(half_ints, metric_inv, occ_energy, vir_energy):
    groups, blocks = lax.axis_size("aux"), lax.axis_size("blk")
    shard, vir = half_ints.shape[1:]
    naux = metric_inv.shape[1]
    tile = shard if shard % 128 == 0 else naux // 4
    pairs = groups // 2
    parts = 4 if shard % 128 == 0 else 1
    dma = pltpu.SemaphoreType.DMA
    return pl.pallas_call(
        functools.partial(kernel, blocks, groups, tile),
        out_shape=jax.ShapeDtypeStruct(half_ints.shape, jnp.bfloat16),
        in_specs=[
            pl.BlockSpec(memory_space=pl.ANY),
            pl.BlockSpec(memory_space=pl.ANY),
            pl.BlockSpec(memory_space=pltpu.SMEM),
            pl.BlockSpec(memory_space=pltpu.VMEM),
        ],
        out_specs=pl.BlockSpec(memory_space=pl.ANY),
        scratch_shapes=[
            pltpu.VMEM((CYCLE, naux, vir), jnp.bfloat16),
            pltpu.VMEM((naux, naux), jnp.bfloat16),
            pltpu.VMEM((naux, naux), jnp.bfloat16),
            pltpu.VMEM((CYCLE, naux, vir), jnp.bfloat16),
            pltpu.VMEM((vir, naux), jnp.bfloat16),
            pltpu.VMEM((vir, vir), jnp.float32),
            pltpu.VMEM((vir, vir), jnp.float32),
            pltpu.VMEM((naux, vir), jnp.float32),
            pltpu.VMEM((naux, vir), jnp.bfloat16),
            pltpu.VMEM((naux, vir), jnp.bfloat16),
            dma((groups,)), dma((groups,)), dma(()), dma((groups,)), dma((groups,)), dma((CYCLE, groups)),
            dma((2,)), dma((2,)),
            dma((pairs, parts)), dma((pairs, parts)), dma((pairs, parts)), dma((pairs, parts)), dma((pairs,)), dma((pairs,)),
            dma(()), dma((groups,)), dma((groups,)),
        ],
        compiler_params=pltpu.CompilerParams(
            collective_id=0, has_side_effects=True, vmem_limit_bytes=56 * 2**20
        ),
    )(half_ints, metric_inv, occ_energy, vir_energy)


def solution(mesh):
    placed = (P("blk", "aux", None), P("aux", None), P(), P())
    return jax.shard_map(
        local, mesh=mesh, in_specs=placed, out_specs=P("blk", "aux", None), check_vma=False
    )
```

```python
import functools

import jax
import jax.numpy as jnp
from jax import lax
from jax.experimental import pallas as pl
from jax.experimental.pallas import tpu as pltpu
from jax.sharding import PartitionSpec as P

MESH = pl.DeviceIdType.MESH


def kernel(
    blocks, groups, tile,
    ints_ref, metric_ref, occ_ref, vir_ref,
    out_ref,
    near, far, metric, metric_t, fit_a, fit_b, fit_t, amp_a, amp_b, gap, pair_sum, dens, dens_b, gam, occ, levels,
    occ_sem, vir_sem, h_send, h_recv, d_send, z_send, w_send, ring_recv, f_send, f_recv,
    m1_send, m1_recv, m2_send, m2_recv, m3_send, m3_recv, own_sem, g_send, g_recv,
):
    shard = ints_ref.shape[1]
    half = shard // 2
    parts = 4 if half % 64 == 0 else 1
    part = half // parts
    naux = metric_ref.shape[1]
    vir = ints_ref.shape[2]
    tiles = naux // tile
    pairs = groups // 2
    b, g = lax.axis_index("blk"), lax.axis_index("aux")
    x, core, h = b % 2, g % 2, g // 2
    plane, mate, ahead = b - x, g + 1 - 2 * core, (b + 2) % blocks
    across = b + 1 - 2 * x
    own_b, own_c = plane + core, g - core + x
    f32 = jnp.float32

    def rows(p):
        return pl.ds(pl.multiple_of(p * shard, shard), shard)

    def slab(p, which, n):
        return pl.ds(pl.multiple_of(p * shard + which * half + n * part, part), part)

    def span(q):
        return pl.ds(pl.multiple_of(q * tile, tile), tile)

    def width(hv):
        return min(naux, -(-2 * shard * (hv + 1) // tile) * tile)

    def remote(src, dst, send, recv, device):
        return pltpu.make_async_remote_copy(
            src_ref=src, dst_ref=dst, send_sem=send, recv_sem=recv,
            device_id=device, device_id_type=MESH,
        )

    def landed(dst, recv):
        pltpu.make_async_copy(dst, dst, recv).wait()

    first, second = pl.ds(0, vir), pl.ds(vir, vir)
    occ_copy = pltpu.make_async_copy(occ_ref, occ, occ_sem)
    vir_copy = pltpu.make_async_copy(vir_ref, levels, vir_sem)
    barrier = pltpu.get_barrier_semaphore()
    for xx in range(2):
        for gg in range(groups):
            @pl.when((plane + xx != b) | (gg != g))
            def _():
                pl.semaphore_signal(barrier, inc=1, device_id=(plane + xx, gg), device_id_type=MESH)
    for bb in (ahead, (b + blocks - 2) % blocks):
        for gg in (g, mate):
            pl.semaphore_signal(barrier, inc=1, device_id=(bb, gg), device_id_type=MESH)
    pl.semaphore_wait(barrier, 2 * groups + 3)

    def ints_copy(c):
        return remote(
            ints_ref.at[c], near.at[rows(g), first], h_send.at[c], h_recv.at[g],
            (plane + c % 2, c - c % 2 + x),
        )

    def to_self(c):
        return (core == x) & (c == own_c)

    order = [(2 * ((h + r) % pairs) + par) for r in range(pairs) for par in range(2)]
    tail_first = [groups - 2] + [p for p in range(groups - 1, -1, -1) if p != groups - 2]

    def d_copy():
        return remote(
            ints_ref.at[own_c], near.at[rows(g), second], d_send, ring_recv.at[0, g], (ahead, own_c)
        )

    d_copy().start()
    for c in order:
        @pl.when(jnp.logical_not(to_self(c)))
        def _():
            ints_copy(c).start()

        @pl.when(to_self(c))
        def _():
            pltpu.make_async_copy(ints_ref.at[c], near.at[rows(g), first], h_recv.at[g]).start()

    own_metric = pltpu.make_async_copy(metric_ref, metric.at[rows(g)], own_sem)
    own_metric.start()

    def m1_copy(hv, r, n):
        return remote(
            metric_ref.at[slab(0, x, n), pl.ds(0, width(hv))],
            metric.at[slab(g, x, n), pl.ds(0, width(hv))],
            m1_send.at[r, n], m1_recv.at[hv, n],
            (b, 2 * ((h + r) % pairs) + core),
        )

    def m3_own(hv):
        return remote(
            metric_ref.at[:, pl.ds(0, width(hv))], metric.at[rows(g), pl.ds(0, width(hv))],
            m3_send.at[hv], m3_recv.at[hv], (b, mate),
        )

    def m2_copy(hv, n):
        piece = metric.at[slab(2 * hv + core, x, n), pl.ds(0, width(hv))]
        return remote(piece, piece, m2_send.at[hv, n], m2_recv.at[hv, n], (across, g))

    def m3_copy(hv):
        piece = metric.at[rows(2 * hv + core), pl.ds(0, width(hv))]
        return remote(piece, piece, m3_send.at[hv], m3_recv.at[hv], (b, mate))

    for hv in range(pairs):
        @pl.when(h == hv)
        def _():
            for r in range(1, pairs):
                for n in range(parts):
                    m1_copy(hv, r, n).start()
            m3_own(hv).start()

    def z_copy(p):
        return remote(near.at[rows(p), first], near.at[rows(p), second], z_send.at[p], ring_recv.at[0, p], (ahead, g))

    def w_copy(p):
        return remote(near.at[rows(p), second], far.at[rows(p)], w_send.at[p], ring_recv.at[1, p], (ahead, mate))

    def sent_up(p):
        return jnp.logical_not((core == x) & (p // 2 == h))

    def f_copy_all(q):
        return remote(fit_a.at[span(q)], fit_b.at[span(q)], f_send.at[q], f_recv.at[q], (b, mate))

    def f_copy_one(q):
        return remote(
            fit_a.at[span(q), second], fit_b.at[span(q), first], f_send.at[q], f_recv.at[q], (b, mate)
        )

    occ_copy.start()
    vir_copy.start()
    vir_copy.wait()
    occ_copy.wait()
    level = jnp.broadcast_to(levels[...], (vir, vir))
    gap[...] = level + level.T

    for p in order:
        landed(near.at[rows(p), first], h_recv.at[p])

        @pl.when(sent_up(p))
        def _():
            z_copy(p).start()

    for hv in range(pairs):
        @pl.when(h != hv)
        def _():
            for n in range(parts):
                landed(metric.at[slab(2 * hv + core, x, n), pl.ds(0, width(hv))], m1_recv.at[hv, n])
                m2_copy(hv, n).start()
    for hv in range(pairs):
        @pl.when(h != hv)
        def _():
            for n in range(parts):
                landed(metric.at[slab(2 * hv + core, 1 - x, n), pl.ds(0, width(hv))], m2_recv.at[hv, n])
            m3_copy(hv).start()

    for p in tail_first:
        landed(near.at[rows(p), second], ring_recv.at[0, p])

        @pl.when(core == 1)
        def _():
            w_copy(p).start()

    own_metric.wait()
    for hv in range(pairs):
        landed(metric.at[rows(2 * hv + 1 - core), pl.ds(0, width(hv))], m3_recv.at[hv])

    @pl.loop(0, tiles)
    def _(p):
        @pl.loop(0, p + 1)
        def _(q):
            metric_t[span(q), span(p)] = metric[span(p), span(q)].T

    own_energy = occ[own_b * groups + own_c]

    def amplitude_of(pair, role):
        energy = own_energy + occ[(own_b + blocks - role) % blocks * groups + own_c]
        return ((2.0 * pair.T - pair) / (energy - gap[...])).astype(amp_a.dtype)

    for q in range(tiles):
        low = q * tile
        fit_a[low:low + tile, :] = jnp.dot(
            metric_t[low:low + tile, low:], near[low:, :], preferred_element_type=f32,
        ).astype(fit_a.dtype)

        @pl.when(core == 0)
        def _():
            f_copy_all(q).start()

        @pl.when(core == 1)
        def _():
            f_copy_one(q).start()

        fit_t[:, low:low + tile] = fit_a[low:low + tile, :vir].T

    pair = jnp.dot(fit_t[...], fit_a[...], preferred_element_type=f32)
    amp_a[:vir, :] = amplitude_of(pair[:, :vir], 0)
    amp_a[vir:, :] = amplitude_of(pair[:, vir:], 2)
    dens[...] = jnp.dot(fit_a[...], amp_a[...], preferred_element_type=f32)

    @pl.when(core == 1)
    def _():
        for q in range(tiles):
            landed(fit_b.at[span(q)], f_recv.at[q])
        pair = jnp.dot(fit_t[...], fit_b[...], preferred_element_type=f32)
        amp_b[:vir, :] = amplitude_of(pair[:, :vir], 1)
        amp_b[vir:, :] = amplitude_of(pair[:, vir:], 3)

    @pl.when(core == 0)
    def _():
        for q in range(tiles):
            landed(fit_b.at[span(q), first], f_recv.at[q])
        pair = jnp.dot(fit_t[...], fit_b[:, :vir], preferred_element_type=f32)
        amp_b[:vir, :] = amplitude_of(pair, 1)
        dens[...] += jnp.dot(fit_b[:, :vir], amp_b[:vir, :], preferred_element_type=f32)
        for q in reversed(range(tiles)):
            low = q * tile
            for p in reversed(range(low // shard, (low + tile) // shard)):
                landed(far.at[rows(p)], ring_recv.at[1, p])
            fit_b[low:low + tile, vir:] = jnp.dot(
                metric_t[low:low + tile, low:], far[low:, :], preferred_element_type=f32,
            ).astype(fit_b.dtype)
            part_sum = jnp.dot(
                fit_t[:, low:low + tile], fit_b[low:low + tile, vir:], preferred_element_type=f32
            )
            if q == tiles - 1:
                pair_sum[...] = part_sum
            else:
                pair_sum[...] += part_sum
        amp_b[vir:, :] = amplitude_of(pair_sum[...], 3)

    def g_copy(p):
        return remote(gam.at[rows(p)], out_ref.at[own_c], g_send.at[p], g_recv.at[own_c], (own_b, p))

    def g_self(p):
        return (core == x) & (g == p)

    for t in range(tiles):
        low = t * tile

        @pl.when(core == 0)
        def _():
            total = dens[low:low + tile, :] + jnp.dot(
                fit_b[low:low + tile, vir:], amp_b[vir:, :], preferred_element_type=f32
            )
            dens_b[low:low + tile, :] = total.astype(dens_b.dtype)

        @pl.when(core == 1)
        def _():
            total = dens[low:low + tile, :] + jnp.dot(
                fit_b[low:low + tile, :], amp_b[...], preferred_element_type=f32
            )
            dens_b[low:low + tile, :] = total.astype(dens_b.dtype)

        gam[low:low + tile, :] = jnp.dot(
            metric[low:low + tile, :low + tile], dens_b[:low + tile, :],
            preferred_element_type=f32,
        ).astype(gam.dtype)
        for p in range(low // shard, (low + tile) // shard):
            @pl.when(jnp.logical_not(g_self(p)))
            def _():
                g_copy(p).start()

            @pl.when(g_self(p))
            def _():
                pltpu.make_async_copy(gam.at[rows(p)], out_ref.at[own_c], g_recv.at[own_c]).start()

    d_copy().wait_send()
    for c in range(groups):
        @pl.when(jnp.logical_not(to_self(c)))
        def _():
            ints_copy(c).wait_send()

        @pl.when(sent_up(c))
        def _():
            z_copy(c).wait_send()

        @pl.when(core == 1)
        def _():
            w_copy(c).wait_send()

        @pl.when(jnp.logical_not(g_self(c)))
        def _():
            g_copy(c).wait_send()

    for q in range(tiles):
        @pl.when(core == 0)
        def _():
            f_copy_all(q).wait_send()

        @pl.when(core == 1)
        def _():
            f_copy_one(q).wait_send()

    for hv in range(pairs):
        @pl.when(h == hv)
        def _():
            for r in range(1, pairs):
                for n in range(parts):
                    m1_copy(hv, r, n).wait_send()
            m3_own(hv).wait_send()

        @pl.when(h != hv)
        def _():
            for n in range(parts):
                m2_copy(hv, n).wait_send()
            m3_copy(hv).wait_send()
    for c in range(groups):
        landed(out_ref.at[c], g_recv.at[c])


def local(half_ints, metric_inv, occ_energy, vir_energy):
    groups, blocks = lax.axis_size("aux"), lax.axis_size("blk")
    shard, vir = half_ints.shape[1:]
    naux = metric_inv.shape[1]
    tile = shard if shard % 128 == 0 else naux // 4
    pairs, tiles = groups // 2, naux // tile
    parts = 4 if shard % 128 == 0 else 1
    dma = pltpu.SemaphoreType.DMA
    return pl.pallas_call(
        functools.partial(kernel, blocks, groups, tile),
        out_shape=jax.ShapeDtypeStruct(half_ints.shape, jnp.bfloat16),
        in_specs=[
            pl.BlockSpec(memory_space=pl.ANY),
            pl.BlockSpec(memory_space=pl.ANY),
            pl.BlockSpec(memory_space=pl.ANY),
            pl.BlockSpec(memory_space=pl.ANY),
        ],
        out_specs=pl.BlockSpec(memory_space=pl.ANY),
        scratch_shapes=[
            pltpu.VMEM((naux, 2 * vir), jnp.bfloat16),
            pltpu.VMEM((naux, vir), jnp.bfloat16),
            pltpu.VMEM((naux, naux), jnp.bfloat16),
            pltpu.VMEM((naux, naux), jnp.bfloat16),
            pltpu.VMEM((naux, 2 * vir), jnp.bfloat16),
            pltpu.VMEM((naux, 2 * vir), jnp.bfloat16),
            pltpu.VMEM((vir, naux), jnp.bfloat16),
            pltpu.VMEM((2 * vir, vir), jnp.bfloat16),
            pltpu.VMEM((2 * vir, vir), jnp.bfloat16),
            pltpu.VMEM((vir, vir), jnp.float32),
            pltpu.VMEM((vir, vir), jnp.float32),
            pltpu.VMEM((naux, vir), jnp.float32),
            pltpu.VMEM((naux, vir), jnp.bfloat16),
            pltpu.VMEM((naux, vir), jnp.bfloat16),
            pltpu.SMEM(occ_energy.shape, jnp.float32),
            pltpu.VMEM(vir_energy.shape, jnp.float32),
            dma(()), dma(()),
            dma((groups,)), dma((groups,)), dma(()), dma((groups,)), dma((groups,)), dma((2, groups)),
            dma((tiles,)), dma((tiles,)),
            dma((pairs, parts)), dma((pairs, parts)), dma((pairs, parts)), dma((pairs, parts)), dma((pairs,)), dma((pairs,)),
            dma(()), dma((groups,)), dma((groups,)),
        ],
        compiler_params=pltpu.CompilerParams(
            collective_id=0, has_side_effects=True, vmem_limit_bytes=56 * 2**20
        ),
    )(half_ints, metric_inv, occ_energy, vir_energy)


def solution(mesh):
    placed = (P("blk", "aux", None), P("aux", None), P(), P())
    return jax.shard_map(
        local, mesh=mesh, in_specs=placed, out_specs=P("blk", "aux", None), check_vma=False
    )
```

```python
import functools

import jax
import jax.numpy as jnp
from jax import lax
from jax.experimental import pallas as pl
from jax.experimental.pallas import tpu as pltpu
from jax.sharding import PartitionSpec as P

MESH = pl.DeviceIdType.MESH


def kernel(
    blocks, groups, tile,
    ints_ref, metric_ref, occ_ref, vir_ref,
    out_ref,
    near, far, metric, metric_t, fit_a, fit_b, fit_t, amp_a, amp_b, gap, pair_sum, dens, dens_b, gam, occ, levels,
    occ_sem, vir_sem, go, h_send, h_recv, d_send, z_send, w_send, ring_recv, f_send, f_recv,
    m1_send, m1_recv, m2_send, m2_recv, m3_send, m3_recv, mo_send, mo_recv, own_sem, g_send, g_recv,
):
    shard = ints_ref.shape[1]
    half = shard // 2
    parts = 6 if half % 96 == 0 else 1
    part = half // parts
    naux = metric_ref.shape[1]
    vir = ints_ref.shape[2]
    tiles = naux // tile
    pairs = groups // 2
    b, g = lax.axis_index("blk"), lax.axis_index("aux")
    x, core, h = b % 2, g % 2, g // 2
    plane, mate, ahead = b - x, g + 1 - 2 * core, (b + 2) % blocks
    across = b + 1 - 2 * x
    own_b, own_c = plane + core, g - core + x
    f32 = jnp.float32

    def rows(p):
        return pl.ds(pl.multiple_of(p * shard, shard), shard)

    def span(q):
        return pl.ds(pl.multiple_of(q * tile, tile), tile)

    def wide(p, n):
        return min(naux, -(-(p * shard + 2 * (n + 1) * part) // 128) * 128)

    def tile_end(p):
        return (p * shard // tile + 1) * tile

    def remote(src, dst, send, recv, device):
        return pltpu.make_async_remote_copy(
            src_ref=src, dst_ref=dst, send_sem=send, recv_sem=recv,
            device_id=device, device_id_type=MESH,
        )

    def landed(dst, recv):
        pltpu.make_async_copy(dst, dst, recv).wait()

    first, second = pl.ds(0, vir), pl.ds(vir, vir)
    occ_copy = pltpu.make_async_copy(occ_ref, occ, occ_sem)
    vir_copy = pltpu.make_async_copy(vir_ref, levels, vir_sem)
    barrier = pltpu.get_barrier_semaphore()
    for xx in range(2):
        for gg in range(groups):
            @pl.when((plane + xx != b) | (gg != g))
            def _():
                pl.semaphore_signal(barrier, inc=1, device_id=(plane + xx, gg), device_id_type=MESH)
    for bb in (ahead, (b + blocks - 2) % blocks):
        for gg in (g, mate):
            pl.semaphore_signal(barrier, inc=1, device_id=(bb, gg), device_id_type=MESH)
    pl.semaphore_wait(barrier, 2 * groups + 3)

    def ints_copy(c):
        return remote(
            ints_ref.at[c], near.at[rows(g), first], h_send.at[c], h_recv.at[g],
            (plane + c % 2, c - c % 2 + x),
        )

    def to_self(c):
        return (core == x) & (c == own_c)

    order = [(2 * ((h + r) % pairs) + par) for r in range(pairs) for par in range(2)]
    last = 2 * ((h + pairs - 1) % pairs) + 1 - x
    tail_first = [groups - 2] + [p for p in range(groups - 1, -1, -1) if p != groups - 2]

    def d_copy():
        return remote(
            ints_ref.at[own_c], near.at[rows(g), second], d_send, ring_recv.at[0, g], (ahead, own_c)
        )

    d_copy().start()
    for c in order:
        @pl.when(jnp.logical_not(to_self(c)))
        def _():
            ints_copy(c).start()

        @pl.when(to_self(c))
        def _():
            pltpu.make_async_copy(ints_ref.at[c], near.at[rows(g), first], h_recv.at[g]).start()

    own_metric = pltpu.make_async_copy(metric_ref, metric.at[rows(g)], own_sem)
    own_metric.start()

    def at_home(act):
        for hv in range(pairs):
            for cc in range(2):
                @pl.when((h == hv) & (core == cc))
                def _():
                    act(hv, 2 * hv + cc)

    def away(act):
        for hv in range(pairs):
            for cc in range(2):
                @pl.when((h != hv) & (core == cc))
                def _():
                    act(hv, 2 * hv + cc)

    def band(p, which, n):
        low = pl.multiple_of(p * shard + (2 * n + which) * part, part)
        return metric.at[pl.ds(low, part), pl.ds(0, wide(p, n))]

    def m1_copy(hv, p, r, n):
        low = pl.multiple_of((2 * n + x) * part, part)
        return remote(
            metric_ref.at[pl.ds(low, part), pl.ds(0, wide(p, n))], band(p, x, n),
            m1_send.at[r, n], m1_recv.at[hv, n], (b, 2 * ((h + r) % pairs) + core),
        )

    def m2_copy(hv, p, n):
        return remote(band(p, x, n), band(p, x, n), m2_send.at[hv, n], m2_recv.at[hv, n], (across, g))

    def m3_copy(hv, p, own, n):
        which = x if own else 1 - x
        return remote(
            band(p, which, n), band(p, which, n),
            m3_send.at[hv, which, n], m3_recv.at[hv, which, n], (b, mate),
        )

    def home_rows(p):
        return metric.at[pl.ds(p * shard, shard), pl.ds(0, tile_end(p))]

    def mo_copy(p):
        return remote(metric_ref.at[:, pl.ds(0, tile_end(p))], home_rows(p), mo_send, mo_recv, (b, mate))

    @at_home
    def _(hv, p):
        mo_copy(p).start()

    for p in range(groups):
        @pl.when(p // 2 != h)
        def _():
            for n in range(parts):
                if wide(p, n) < tile_end(p):
                    low = p * shard + 2 * n * part
                    fill = jnp.zeros((2 * part, tile_end(p) - wide(p, n)), metric.dtype)
                    metric[low:low + 2 * part, wide(p, n):tile_end(p)] = fill

    def m1_step(n):
        @away
        def _(hv, p):
            landed(band(p, x, n), m1_recv.at[hv, n])
            m2_copy(hv, p, n).start()
            m3_copy(hv, p, True, n).start()

    def m2_step(n):
        @away
        def _(hv, p):
            landed(band(p, 1 - x, n), m2_recv.at[hv, n])
            m3_copy(hv, p, False, n).start()

    def z_copy(p):
        return remote(near.at[rows(p), first], near.at[rows(p), second], z_send.at[p], ring_recv.at[0, p], (ahead, g))

    def w_copy(p):
        return remote(near.at[rows(p), second], far.at[rows(p)], w_send.at[p], ring_recv.at[1, p], (ahead, mate))

    def sent_up(p):
        return jnp.logical_not((core == x) & (p // 2 == h))

    def f_copy_all(q):
        return remote(fit_a.at[span(q)], fit_b.at[span(q)], f_send.at[q], f_recv.at[q], (b, mate))

    def f_copy_one(q):
        return remote(
            fit_a.at[span(q), second], fit_b.at[span(q), first], f_send.at[q], f_recv.at[q], (b, mate)
        )

    occ_copy.start()
    vir_copy.start()
    vir_copy.wait()
    occ_copy.wait()
    level = jnp.broadcast_to(levels[...], (vir, vir))
    gap[...] = level + level.T

    own_metric.wait()

    @at_home
    def _(hv, p):
        landed(home_rows(p + 1 - 2 * (p % 2)), mo_recv)

    def turn(p):
        @pl.loop(0, p + 1)
        def _(q):
            metric_t[span(q), span(p)] = metric[span(p), span(q)].T

    if tile == shard:
        turn(2 * h)
        turn(2 * h + 1)

    def pass_own(p):
        landed(near.at[rows(p), first], h_recv.at[p])

        @pl.when(sent_up(p))
        def _():
            z_copy(p).start()

    def pass_on(p):
        landed(near.at[rows(p), second], ring_recv.at[0, p])

        @pl.when(core == 1)
        def _():
            w_copy(p).start()

    for p in order[:2]:
        pass_own(p)

    @at_home
    def _(hv, p):
        for n in range(parts // 2):
            for r in range(1, pairs):
                m1_copy(hv, p, r, n).start()

    for p in order[2:3]:
        pass_own(p)
    ints_copy(last).wait_send()

    @at_home
    def _(hv, p):
        for n in range(parts // 2, parts):
            for r in range(1, pairs):
                m1_copy(hv, p, r, n).start()

    for p in order[3:]:
        pass_own(p)
    for n in range(parts):
        m1_step(n)
        if n >= 2:
            m2_step(n - 2)
    @pl.when(core == 0)
    def _():
        for p in range(groups):
            @pl.when(sent_up(p))
            def _():
                z_copy(p).wait_send()
        pl.semaphore_signal(go, inc=1, device_id=(b, mate), device_id_type=MESH)

    @pl.when(core == 1)
    def _():
        pl.semaphore_wait(go, 1)

    pass_on(tail_first[0])
    for n in range(max(parts - 2, 0), parts):
        m2_step(n)
    for p in tail_first[1:]:
        pass_on(p)

    @away
    def _(hv, p):
        other = p + 1 - 2 * (p % 2)
        for n in range(parts):
            landed(band(other, 0, n), m3_recv.at[hv, 0, n])
            landed(band(other, 1, n), m3_recv.at[hv, 1, n])

    if tile == shard:
        for r in range(1, pairs):
            turn(2 * ((h + r) % pairs))
            turn(2 * ((h + r) % pairs) + 1)
    else:
        pl.loop(0, tiles)(turn)

    own_energy = occ[own_b * groups + own_c]

    def amplitude_of(pair, role):
        energy = own_energy + occ[(own_b + blocks - role) % blocks * groups + own_c]
        return ((2.0 * pair.T - pair) / (energy - gap[...])).astype(amp_a.dtype)

    for q in range(tiles):
        low = q * tile
        fit_a[low:low + tile, :] = jnp.dot(
            metric_t[low:low + tile, low:], near[low:, :], preferred_element_type=f32,
        ).astype(fit_a.dtype)

        @pl.when(core == 0)
        def _():
            f_copy_all(q).start()

        @pl.when(core == 1)
        def _():
            f_copy_one(q).start()

        fit_t[:, low:low + tile] = fit_a[low:low + tile, :vir].T

    pair = jnp.dot(fit_t[...], fit_a[...], preferred_element_type=f32)
    amp_a[:vir, :] = amplitude_of(pair[:, :vir], 0)
    amp_a[vir:, :] = amplitude_of(pair[:, vir:], 2)
    dens[...] = jnp.dot(fit_a[...], amp_a[...], preferred_element_type=f32)

    @pl.when(core == 1)
    def _():
        for q in range(tiles):
            landed(fit_b.at[span(q)], f_recv.at[q])
        pair = jnp.dot(fit_t[...], fit_b[...], preferred_element_type=f32)
        amp_b[:vir, :] = amplitude_of(pair[:, :vir], 1)
        amp_b[vir:, :] = amplitude_of(pair[:, vir:], 3)

    @pl.when(core == 0)
    def _():
        for q in range(tiles):
            landed(fit_b.at[span(q), first], f_recv.at[q])
        pair = jnp.dot(fit_t[...], fit_b[:, :vir], preferred_element_type=f32)
        amp_b[:vir, :] = amplitude_of(pair, 1)
        dens[...] += jnp.dot(fit_b[:, :vir], amp_b[:vir, :], preferred_element_type=f32)
        for q in reversed(range(tiles)):
            low = q * tile
            for p in reversed(range(low // shard, (low + tile) // shard)):
                landed(far.at[rows(p)], ring_recv.at[1, p])
            fit_b[low:low + tile, vir:] = jnp.dot(
                metric_t[low:low + tile, low:], far[low:, :], preferred_element_type=f32,
            ).astype(fit_b.dtype)
            part_sum = jnp.dot(
                fit_t[:, low:low + tile], fit_b[low:low + tile, vir:], preferred_element_type=f32
            )
            if q == tiles - 1:
                pair_sum[...] = part_sum
            else:
                pair_sum[...] += part_sum
        amp_b[vir:, :] = amplitude_of(pair_sum[...], 3)

    def g_copy(p):
        return remote(gam.at[rows(p)], out_ref.at[own_c], g_send.at[p], g_recv.at[own_c], (own_b, p))

    def g_self(p):
        return (core == x) & (g == p)

    for t in range(tiles):
        low = t * tile

        @pl.when(core == 0)
        def _():
            total = dens[low:low + tile, :] + jnp.dot(
                fit_b[low:low + tile, vir:], amp_b[vir:, :], preferred_element_type=f32
            )
            dens_b[low:low + tile, :] = total.astype(dens_b.dtype)

        @pl.when(core == 1)
        def _():
            total = dens[low:low + tile, :] + jnp.dot(
                fit_b[low:low + tile, :], amp_b[...], preferred_element_type=f32
            )
            dens_b[low:low + tile, :] = total.astype(dens_b.dtype)

        gam[low:low + tile, :] = jnp.dot(
            metric[low:low + tile, :low + tile], dens_b[:low + tile, :],
            preferred_element_type=f32,
        ).astype(gam.dtype)
        for p in range(low // shard, (low + tile) // shard):
            @pl.when(jnp.logical_not(g_self(p)))
            def _():
                g_copy(p).start()

            @pl.when(g_self(p))
            def _():
                pltpu.make_async_copy(gam.at[rows(p)], out_ref.at[own_c], g_recv.at[own_c]).start()

    d_copy().wait_send()
    for c in range(groups):
        @pl.when(jnp.logical_not(to_self(c)) & (c != last))
        def _():
            ints_copy(c).wait_send()

        @pl.when(sent_up(c) & (core == 1))
        def _():
            z_copy(c).wait_send()

        @pl.when(core == 1)
        def _():
            w_copy(c).wait_send()

        @pl.when(jnp.logical_not(g_self(c)))
        def _():
            g_copy(c).wait_send()

    for q in range(tiles):
        @pl.when(core == 0)
        def _():
            f_copy_all(q).wait_send()

        @pl.when(core == 1)
        def _():
            f_copy_one(q).wait_send()

    @at_home
    def _(hv, p):
        for n in range(parts):
            for r in range(1, pairs):
                m1_copy(hv, p, r, n).wait_send()
        mo_copy(p).wait_send()

    @away
    def _(hv, p):
        for n in range(parts):
            m2_copy(hv, p, n).wait_send()
            m3_copy(hv, p, True, n).wait_send()
            m3_copy(hv, p, False, n).wait_send()

    for c in range(groups):
        landed(out_ref.at[c], g_recv.at[c])


def local(half_ints, metric_inv, occ_energy, vir_energy):
    groups, blocks = lax.axis_size("aux"), lax.axis_size("blk")
    shard, vir = half_ints.shape[1:]
    naux = metric_inv.shape[1]
    tile = shard if shard % 128 == 0 else naux // 4
    pairs, tiles = groups // 2, naux // tile
    parts = 6 if shard % 192 == 0 else 1
    dma = pltpu.SemaphoreType.DMA
    return pl.pallas_call(
        functools.partial(kernel, blocks, groups, tile),
        out_shape=jax.ShapeDtypeStruct(half_ints.shape, jnp.bfloat16),
        in_specs=[
            pl.BlockSpec(memory_space=pl.ANY),
            pl.BlockSpec(memory_space=pl.ANY),
            pl.BlockSpec(memory_space=pl.ANY),
            pl.BlockSpec(memory_space=pl.ANY),
        ],
        out_specs=pl.BlockSpec(memory_space=pl.ANY),
        scratch_shapes=[
            pltpu.VMEM((naux, 2 * vir), jnp.bfloat16),
            pltpu.VMEM((naux, vir), jnp.bfloat16),
            pltpu.VMEM((naux, naux), jnp.bfloat16),
            pltpu.VMEM((naux, naux), jnp.bfloat16),
            pltpu.VMEM((naux, 2 * vir), jnp.bfloat16),
            pltpu.VMEM((naux, 2 * vir), jnp.bfloat16),
            pltpu.VMEM((vir, naux), jnp.bfloat16),
            pltpu.VMEM((2 * vir, vir), jnp.bfloat16),
            pltpu.VMEM((2 * vir, vir), jnp.bfloat16),
            pltpu.VMEM((vir, vir), jnp.float32),
            pltpu.VMEM((vir, vir), jnp.float32),
            pltpu.VMEM((naux, vir), jnp.float32),
            pltpu.VMEM((naux, vir), jnp.bfloat16),
            pltpu.VMEM((naux, vir), jnp.bfloat16),
            pltpu.SMEM(occ_energy.shape, jnp.float32),
            pltpu.VMEM(vir_energy.shape, jnp.float32),
            dma(()), dma(()), pltpu.SemaphoreType.REGULAR,
            dma((groups,)), dma((groups,)), dma(()), dma((groups,)), dma((groups,)), dma((2, groups)),
            dma((tiles,)), dma((tiles,)),
            dma((pairs, parts)), dma((pairs, parts)), dma((pairs, parts)), dma((pairs, parts)),
            dma((pairs, 2, parts)), dma((pairs, 2, parts)), dma(()), dma(()),
            dma(()), dma((groups,)), dma((groups,)),
        ],
        compiler_params=pltpu.CompilerParams(
            collective_id=0, has_side_effects=True, vmem_limit_bytes=56 * 2**20
        ),
    )(half_ints, metric_inv, occ_energy, vir_energy)


def solution(mesh):
    placed = (P("blk", "aux", None), P("aux", None), P(), P())
    return jax.shard_map(
        local, mesh=mesh, in_specs=placed, out_specs=P("blk", "aux", None), check_vma=False
    )
```

```python
import functools

import jax
import jax.numpy as jnp
from jax import lax
from jax.experimental import pallas as pl
from jax.experimental.pallas import tpu as pltpu
from jax.sharding import PartitionSpec as P

MESH = pl.DeviceIdType.MESH


def kernel(
    blocks, groups, tile,
    ints_ref, metric_ref, occ_ref, vir_ref,
    out_ref,
    near, far, metric, metric_t, fit_a, fit_b, fit_t, amp_a, amp_b, gap, pair_sum, dens, dens_b, gam, occ, levels,
    occ_sem, vir_sem, go, h_send, h_recv, d_send, z_send, w_send, ring_recv, far_recv, f_send, f_recv,
    m1_send, m1_recv, m2_send, m2_recv, m3_send, m3_recv, mo_send, mo_recv, own_sem, g_send, g_recv,
):
    shard = ints_ref.shape[1]
    half = shard // 2
    parts = 6 if half % 96 == 0 else 1
    part = half // parts
    naux = metric_ref.shape[1]
    vir = ints_ref.shape[2]
    tiles = naux // tile
    pairs = groups // 2
    b, g = lax.axis_index("blk"), lax.axis_index("aux")
    x, core, h = b % 2, g % 2, g // 2
    plane, mate, ahead = b - x, g + 1 - 2 * core, (b + 2) % blocks
    across = b + 1 - 2 * x
    own_b, own_c = plane + core, g - core + x
    f32 = jnp.float32

    def rows(p):
        return pl.ds(pl.multiple_of(p * shard, shard), shard)

    def span(q):
        return pl.ds(pl.multiple_of(q * tile, tile), tile)

    def wide(p, n):
        return min(naux, -(-(p * shard + 2 * (n + 1) * part) // 128) * 128)

    def tile_end(p):
        return (p * shard // tile + 1) * tile

    def remote(src, dst, send, recv, device):
        return pltpu.make_async_remote_copy(
            src_ref=src, dst_ref=dst, send_sem=send, recv_sem=recv,
            device_id=device, device_id_type=MESH,
        )

    def landed(dst, recv):
        pltpu.make_async_copy(dst, dst, recv).wait()

    first, second = pl.ds(0, vir), pl.ds(vir, vir)
    occ_copy = pltpu.make_async_copy(occ_ref, occ, occ_sem)
    vir_copy = pltpu.make_async_copy(vir_ref, levels, vir_sem)
    barrier = pltpu.get_barrier_semaphore()
    for xx in range(2):
        for gg in range(groups):
            @pl.when((plane + xx != b) | (gg != g))
            def _():
                pl.semaphore_signal(barrier, inc=1, device_id=(plane + xx, gg), device_id_type=MESH)
    for bb in (ahead, (b + blocks - 2) % blocks):
        for gg in (g, mate):
            pl.semaphore_signal(barrier, inc=1, device_id=(bb, gg), device_id_type=MESH)
    pl.semaphore_wait(barrier, 2 * groups + 3)

    def strip(p, k):
        return pl.ds(pl.multiple_of(p * shard + k * half, half), half)

    def ints_copy(c, k):
        return remote(
            ints_ref.at[c, pl.ds(k * half, half)], near.at[strip(g, k), first],
            h_send.at[c, k], h_recv.at[g, k], (plane + c % 2, c - c % 2 + x),
        )

    def to_self(c):
        return (core == x) & (c == own_c)

    order = [(2 * ((h + r) % pairs) + par) for r in range(pairs) for par in range(2)]
    last = 2 * ((h + pairs - 1) % pairs) + 1 - x
    tail_first = [groups - 2] + [p for p in range(groups - 1, -1, -1) if p != groups - 2]

    def d_copy(k):
        return remote(
            ints_ref.at[own_c, pl.ds(k * half, half)], near.at[strip(g, k), second],
            d_send.at[k], ring_recv.at[g, k], (ahead, own_c),
        )

    for k in range(2):
        d_copy(k).start()
    for c in order:
        @pl.when(jnp.logical_not(to_self(c)))
        def _():
            for k in range(2):
                ints_copy(c, k).start()

        @pl.when(to_self(c))
        def _():
            for k in range(2):
                pltpu.make_async_copy(
                    ints_ref.at[c, pl.ds(k * half, half)], near.at[strip(g, k), first], h_recv.at[g, k]
                ).start()

    own_metric = pltpu.make_async_copy(metric_ref, metric.at[rows(g)], own_sem)
    own_metric.start()

    def at_home(act):
        for hv in range(pairs):
            for cc in range(2):
                @pl.when((h == hv) & (core == cc))
                def _():
                    act(hv, 2 * hv + cc)

    def away(act):
        for hv in range(pairs):
            for cc in range(2):
                @pl.when((h != hv) & (core == cc))
                def _():
                    act(hv, 2 * hv + cc)

    def band(p, which, n):
        low = pl.multiple_of(p * shard + (2 * n + which) * part, part)
        return metric.at[pl.ds(low, part), pl.ds(0, wide(p, n))]

    def m1_copy(hv, p, r, n):
        low = pl.multiple_of((2 * n + x) * part, part)
        return remote(
            metric_ref.at[pl.ds(low, part), pl.ds(0, wide(p, n))], band(p, x, n),
            m1_send.at[r, n], m1_recv.at[hv, n], (b, 2 * ((h + r) % pairs) + core),
        )

    def m2_copy(hv, p, n):
        return remote(band(p, x, n), band(p, x, n), m2_send.at[hv, n], m2_recv.at[hv, n], (across, g))

    def m3_copy(hv, p, own, n):
        which = x if own else 1 - x
        return remote(
            band(p, which, n), band(p, which, n),
            m3_send.at[hv, which, n], m3_recv.at[hv, which, n], (b, mate),
        )

    def home_rows(p):
        return metric.at[pl.ds(p * shard, shard), pl.ds(0, tile_end(p))]

    def mo_copy(p):
        return remote(metric_ref.at[:, pl.ds(0, tile_end(p))], home_rows(p), mo_send, mo_recv, (b, mate))

    @at_home
    def _(hv, p):
        mo_copy(p).start()

    for p in range(groups):
        @pl.when(p // 2 != h)
        def _():
            for n in range(parts):
                if wide(p, n) < tile_end(p):
                    low = p * shard + 2 * n * part
                    fill = jnp.zeros((2 * part, tile_end(p) - wide(p, n)), metric.dtype)
                    metric[low:low + 2 * part, wide(p, n):tile_end(p)] = fill

    def m1_step(n):
        @away
        def _(hv, p):
            landed(band(p, x, n), m1_recv.at[hv, n])
            m2_copy(hv, p, n).start()
            m3_copy(hv, p, True, n).start()

    def m2_step(n):
        @away
        def _(hv, p):
            landed(band(p, 1 - x, n), m2_recv.at[hv, n])
            m3_copy(hv, p, False, n).start()

    def z_copy(p, k):
        return remote(
            near.at[strip(p, k), first], near.at[strip(p, k), second],
            z_send.at[p, k], ring_recv.at[p, k], (ahead, g),
        )

    def w_copy(p):
        return remote(near.at[rows(p), second], far.at[rows(p)], w_send.at[p], far_recv.at[p], (ahead, mate))

    def sent_up(p):
        return jnp.logical_not((core == x) & (p // 2 == h))

    def f_copy_all(q):
        return remote(fit_a.at[span(q)], fit_b.at[span(q)], f_send.at[q], f_recv.at[q], (b, mate))

    def f_copy_one(q):
        return remote(
            fit_a.at[span(q), second], fit_b.at[span(q), first], f_send.at[q], f_recv.at[q], (b, mate)
        )

    occ_copy.start()
    vir_copy.start()
    vir_copy.wait()
    occ_copy.wait()
    level = jnp.broadcast_to(levels[...], (vir, vir))
    gap[...] = level + level.T

    own_metric.wait()

    @at_home
    def _(hv, p):
        landed(home_rows(p + 1 - 2 * (p % 2)), mo_recv)

    def turn(p):
        @pl.loop(0, p + 1)
        def _(q):
            metric_t[span(q), span(p)] = metric[span(p), span(q)].T

    if tile == shard:
        turn(2 * h)
        turn(2 * h + 1)

    def pass_own(p):
        for k in range(2):
            landed(near.at[strip(p, k), first], h_recv.at[p, k])

            @pl.when(sent_up(p))
            def _():
                z_copy(p, k).start()

    def pass_on(p):
        for k in range(2):
            landed(near.at[strip(p, k), second], ring_recv.at[p, k])

        @pl.when(core == 1)
        def _():
            w_copy(p).start()

    for p in order[:2]:
        pass_own(p)

    @at_home
    def _(hv, p):
        for n in range(parts // 2):
            for r in range(1, pairs):
                m1_copy(hv, p, r, n).start()

    for p in order[2:3]:
        pass_own(p)
    for k in range(2):
        ints_copy(last, k).wait_send()

    @at_home
    def _(hv, p):
        for n in range(parts // 2, parts):
            for r in range(1, pairs):
                m1_copy(hv, p, r, n).start()

    for p in order[3:]:
        pass_own(p)
    for n in range(parts):
        m1_step(n)
        if n >= 2:
            m2_step(n - 2)
    @pl.when(core == 0)
    def _():
        for p in order[:-1]:
            @pl.when(sent_up(p))
            def _():
                for k in range(2):
                    z_copy(p, k).wait_send()
        pl.semaphore_signal(go, inc=1, device_id=(b, mate), device_id_type=MESH)

    @pl.when(core == 1)
    def _():
        pl.semaphore_wait(go, 1)

    pass_on(tail_first[0])
    for n in range(max(parts - 2, 0), parts):
        m2_step(n)
    for p in tail_first[1:]:
        pass_on(p)

    @away
    def _(hv, p):
        other = p + 1 - 2 * (p % 2)
        for n in range(parts):
            landed(band(other, 0, n), m3_recv.at[hv, 0, n])
            landed(band(other, 1, n), m3_recv.at[hv, 1, n])

    if tile == shard:
        for r in range(1, pairs):
            turn(2 * ((h + r) % pairs))
            turn(2 * ((h + r) % pairs) + 1)
    else:
        pl.loop(0, tiles)(turn)

    own_energy = occ[own_b * groups + own_c]

    def amplitude_of(pair, role):
        energy = own_energy + occ[(own_b + blocks - role) % blocks * groups + own_c]
        return ((2.0 * pair.T - pair) / (energy - gap[...])).astype(amp_a.dtype)

    for q in range(tiles):
        low = q * tile
        fit_a[low:low + tile, :] = jnp.dot(
            metric_t[low:low + tile, low:], near[low:, :], preferred_element_type=f32,
        ).astype(fit_a.dtype)

        @pl.when(core == 0)
        def _():
            f_copy_all(q).start()

        @pl.when(core == 1)
        def _():
            f_copy_one(q).start()

        fit_t[:, low:low + tile] = fit_a[low:low + tile, :vir].T

    pair = jnp.dot(fit_t[...], fit_a[...], preferred_element_type=f32)
    amp_a[:vir, :] = amplitude_of(pair[:, :vir], 0)
    amp_a[vir:, :] = amplitude_of(pair[:, vir:], 2)
    dens[...] = jnp.dot(fit_a[...], amp_a[...], preferred_element_type=f32)

    @pl.when(core == 1)
    def _():
        for q in range(tiles):
            landed(fit_b.at[span(q)], f_recv.at[q])
        pair = jnp.dot(fit_t[...], fit_b[...], preferred_element_type=f32)
        amp_b[:vir, :] = amplitude_of(pair[:, :vir], 1)
        amp_b[vir:, :] = amplitude_of(pair[:, vir:], 3)

    @pl.when(core == 0)
    def _():
        for q in range(tiles):
            landed(fit_b.at[span(q), first], f_recv.at[q])
        pair = jnp.dot(fit_t[...], fit_b[:, :vir], preferred_element_type=f32)
        amp_b[:vir, :] = amplitude_of(pair, 1)
        dens[...] += jnp.dot(fit_b[:, :vir], amp_b[:vir, :], preferred_element_type=f32)
        for q in reversed(range(tiles)):
            low = q * tile
            for p in reversed(range(low // shard, (low + tile) // shard)):
                landed(far.at[rows(p)], far_recv.at[p])
            fit_b[low:low + tile, vir:] = jnp.dot(
                metric_t[low:low + tile, low:], far[low:, :], preferred_element_type=f32,
            ).astype(fit_b.dtype)
            part_sum = jnp.dot(
                fit_t[:, low:low + tile], fit_b[low:low + tile, vir:], preferred_element_type=f32
            )
            if q == tiles - 1:
                pair_sum[...] = part_sum
            else:
                pair_sum[...] += part_sum
        amp_b[vir:, :] = amplitude_of(pair_sum[...], 3)

    def g_copy(p):
        return remote(gam.at[rows(p)], out_ref.at[own_c], g_send.at[p], g_recv.at[own_c], (own_b, p))

    def g_self(p):
        return (core == x) & (g == p)

    for t in range(tiles):
        low = t * tile

        @pl.when(core == 0)
        def _():
            total = dens[low:low + tile, :] + jnp.dot(
                fit_b[low:low + tile, vir:], amp_b[vir:, :], preferred_element_type=f32
            )
            dens_b[low:low + tile, :] = total.astype(dens_b.dtype)

        @pl.when(core == 1)
        def _():
            total = dens[low:low + tile, :] + jnp.dot(
                fit_b[low:low + tile, :], amp_b[...], preferred_element_type=f32
            )
            dens_b[low:low + tile, :] = total.astype(dens_b.dtype)

        gam[low:low + tile, :] = jnp.dot(
            metric[low:low + tile, :low + tile], dens_b[:low + tile, :],
            preferred_element_type=f32,
        ).astype(gam.dtype)
        for p in range(low // shard, (low + tile) // shard):
            @pl.when(jnp.logical_not(g_self(p)))
            def _():
                g_copy(p).start()

            @pl.when(g_self(p))
            def _():
                pltpu.make_async_copy(gam.at[rows(p)], out_ref.at[own_c], g_recv.at[own_c]).start()

    for k in range(2):
        d_copy(k).wait_send()

    @pl.when(core == 0)
    def _():
        for p in order[-1:]:
            for k in range(2):
                z_copy(p, k).wait_send()

    for c in range(groups):
        @pl.when(jnp.logical_not(to_self(c)) & (c != last))
        def _():
            for k in range(2):
                ints_copy(c, k).wait_send()

        @pl.when(sent_up(c) & (core == 1))
        def _():
            for k in range(2):
                z_copy(c, k).wait_send()

        @pl.when(core == 1)
        def _():
            w_copy(c).wait_send()

        @pl.when(jnp.logical_not(g_self(c)))
        def _():
            g_copy(c).wait_send()

    for q in range(tiles):
        @pl.when(core == 0)
        def _():
            f_copy_all(q).wait_send()

        @pl.when(core == 1)
        def _():
            f_copy_one(q).wait_send()

    @at_home
    def _(hv, p):
        for n in range(parts):
            for r in range(1, pairs):
                m1_copy(hv, p, r, n).wait_send()
        mo_copy(p).wait_send()

    @away
    def _(hv, p):
        for n in range(parts):
            m2_copy(hv, p, n).wait_send()
            m3_copy(hv, p, True, n).wait_send()
            m3_copy(hv, p, False, n).wait_send()

    for c in range(groups):
        landed(out_ref.at[c], g_recv.at[c])


def local(half_ints, metric_inv, occ_energy, vir_energy):
    groups, blocks = lax.axis_size("aux"), lax.axis_size("blk")
    shard, vir = half_ints.shape[1:]
    naux = metric_inv.shape[1]
    tile = shard if shard % 128 == 0 else naux // 4
    pairs, tiles = groups // 2, naux // tile
    parts = 6 if shard % 192 == 0 else 1
    dma = pltpu.SemaphoreType.DMA
    return pl.pallas_call(
        functools.partial(kernel, blocks, groups, tile),
        out_shape=jax.ShapeDtypeStruct(half_ints.shape, jnp.bfloat16),
        in_specs=[
            pl.BlockSpec(memory_space=pl.ANY),
            pl.BlockSpec(memory_space=pl.ANY),
            pl.BlockSpec(memory_space=pl.ANY),
            pl.BlockSpec(memory_space=pl.ANY),
        ],
        out_specs=pl.BlockSpec(memory_space=pl.ANY),
        scratch_shapes=[
            pltpu.VMEM((naux, 2 * vir), jnp.bfloat16),
            pltpu.VMEM((naux, vir), jnp.bfloat16),
            pltpu.VMEM((naux, naux), jnp.bfloat16),
            pltpu.VMEM((naux, naux), jnp.bfloat16),
            pltpu.VMEM((naux, 2 * vir), jnp.bfloat16),
            pltpu.VMEM((naux, 2 * vir), jnp.bfloat16),
            pltpu.VMEM((vir, naux), jnp.bfloat16),
            pltpu.VMEM((2 * vir, vir), jnp.bfloat16),
            pltpu.VMEM((2 * vir, vir), jnp.bfloat16),
            pltpu.VMEM((vir, vir), jnp.float32),
            pltpu.VMEM((vir, vir), jnp.float32),
            pltpu.VMEM((naux, vir), jnp.float32),
            pltpu.VMEM((naux, vir), jnp.bfloat16),
            pltpu.VMEM((naux, vir), jnp.bfloat16),
            pltpu.SMEM(occ_energy.shape, jnp.float32),
            pltpu.VMEM(vir_energy.shape, jnp.float32),
            dma(()), dma(()), pltpu.SemaphoreType.REGULAR,
            dma((groups, 2)), dma((groups, 2)), dma((2,)), dma((groups, 2)), dma((groups,)), dma((groups, 2)), dma((groups,)),
            dma((tiles,)), dma((tiles,)),
            dma((pairs, parts)), dma((pairs, parts)), dma((pairs, parts)), dma((pairs, parts)),
            dma((pairs, 2, parts)), dma((pairs, 2, parts)), dma(()), dma(()),
            dma(()), dma((groups,)), dma((groups,)),
        ],
        compiler_params=pltpu.CompilerParams(
            collective_id=0, has_side_effects=True, vmem_limit_bytes=56 * 2**20
        ),
    )(half_ints, metric_inv, occ_energy, vir_energy)


def solution(mesh):
    placed = (P("blk", "aux", None), P("aux", None), P(), P())
    return jax.shard_map(
        local, mesh=mesh, in_specs=placed, out_specs=P("blk", "aux", None), check_vma=False
    )
```

```python
import functools

import jax
import jax.numpy as jnp
from jax import lax
from jax.experimental import pallas as pl
from jax.experimental.pallas import tpu as pltpu
from jax.sharding import PartitionSpec as P

MESH = pl.DeviceIdType.MESH


def kernel(
    blocks, groups, tile,
    ints_ref, metric_ref, occ_ref, vir_ref,
    out_ref,
    near, far, metric, metric_t, fit_a, fit_b, fit_t, amp_a, amp_b, gap, pair_sum, dens, dens_b, gam, occ, levels,
    occ_sem, vir_sem, go, h_send, h_recv, d_send, z_send, w_send, ring_recv, far_recv, f_send, f_recv,
    m1_send, m1_recv, m2_send, m2_recv, m3_send, m3_recv, mo_send, mo_recv, own_sem, g_send, g_recv,
):
    shard = ints_ref.shape[1]
    half = shard // 2
    parts = 6 if half % 96 == 0 else 1
    part = half // parts
    naux = metric_ref.shape[1]
    vir = ints_ref.shape[2]
    tiles = naux // tile
    pairs = groups // 2
    b, g = lax.axis_index("blk"), lax.axis_index("aux")
    x, core, h = b % 2, g % 2, g // 2
    plane, mate, ahead = b - x, g + 1 - 2 * core, (b + 2) % blocks
    across = b + 1 - 2 * x
    own_b, own_c = plane + core, g - core + x
    f32 = jnp.float32

    def rows(p):
        return pl.ds(pl.multiple_of(p * shard, shard), shard)

    def span(q):
        return pl.ds(pl.multiple_of(q * tile, tile), tile)

    def wide(p, n):
        return min(naux, -(-(p * shard + 2 * (n + 1) * part) // 128) * 128)

    def tile_end(p):
        return (p * shard // tile + 1) * tile

    def remote(src, dst, send, recv, device):
        return pltpu.make_async_remote_copy(
            src_ref=src, dst_ref=dst, send_sem=send, recv_sem=recv,
            device_id=device, device_id_type=MESH,
        )

    def landed(dst, recv):
        pltpu.make_async_copy(dst, dst, recv).wait()

    first, second = pl.ds(0, vir), pl.ds(vir, vir)
    occ_copy = pltpu.make_async_copy(occ_ref, occ, occ_sem)
    vir_copy = pltpu.make_async_copy(vir_ref, levels, vir_sem)
    barrier = pltpu.get_barrier_semaphore()
    for xx in range(2):
        for gg in range(groups):
            @pl.when((plane + xx != b) | (gg != g))
            def _():
                pl.semaphore_signal(barrier, inc=1, device_id=(plane + xx, gg), device_id_type=MESH)
    for bb in (ahead, (b + blocks - 2) % blocks):
        for gg in (g, mate):
            pl.semaphore_signal(barrier, inc=1, device_id=(bb, gg), device_id_type=MESH)
    pl.semaphore_wait(barrier, 2 * groups + 3)

    def strip(p, k):
        return pl.ds(pl.multiple_of(p * shard + k * half, half), half)

    def ints_copy(c, k):
        return remote(
            ints_ref.at[c, pl.ds(k * half, half)], near.at[strip(g, k), first],
            h_send.at[c, k], h_recv.at[g, k], (plane + c % 2, c - c % 2 + x),
        )

    def to_self(c):
        return (core == x) & (c == own_c)

    order = [(2 * ((h + r) % pairs) + par) for r in range(pairs) for par in range(2)]
    last = 2 * ((h + pairs - 1) % pairs) + 1 - x
    tail_first = [groups - 2] + [p for p in range(groups - 1, -1, -1) if p != groups - 2]

    def d_copy(k):
        return remote(
            ints_ref.at[own_c, pl.ds(k * half, half)], near.at[strip(g, k), second],
            d_send.at[k], ring_recv.at[g, k], (ahead, own_c),
        )

    for k in range(2):
        d_copy(k).start()
    for c in order:
        @pl.when(jnp.logical_not(to_self(c)))
        def _():
            for k in range(2):
                ints_copy(c, k).start()

        @pl.when(to_self(c))
        def _():
            for k in range(2):
                pltpu.make_async_copy(
                    ints_ref.at[c, pl.ds(k * half, half)], near.at[strip(g, k), first], h_recv.at[g, k]
                ).start()

    own_metric = pltpu.make_async_copy(metric_ref, metric.at[rows(g)], own_sem)
    own_metric.start()

    def at_home(act):
        for hv in range(pairs):
            for cc in range(2):
                @pl.when((h == hv) & (core == cc))
                def _():
                    act(hv, 2 * hv + cc)

    def away(act):
        for hv in range(pairs):
            for cc in range(2):
                @pl.when((h != hv) & (core == cc))
                def _():
                    act(hv, 2 * hv + cc)

    def band(p, which, n):
        low = pl.multiple_of(p * shard + (2 * n + which) * part, part)
        return metric.at[pl.ds(low, part), pl.ds(0, wide(p, n))]

    def m1_copy(hv, p, r, n):
        low = pl.multiple_of((2 * n + x) * part, part)
        return remote(
            metric_ref.at[pl.ds(low, part), pl.ds(0, wide(p, n))], band(p, x, n),
            m1_send.at[r, n], m1_recv.at[hv, n], (b, 2 * ((h + r) % pairs) + core),
        )

    def m2_copy(hv, p, n):
        return remote(band(p, x, n), band(p, x, n), m2_send.at[hv, n], m2_recv.at[hv, n], (across, g))

    def m3_copy(hv, p, own, n):
        which = x if own else 1 - x
        return remote(
            band(p, which, n), band(p, which, n),
            m3_send.at[hv, which, n], m3_recv.at[hv, which, n], (b, mate),
        )

    def home_rows(p):
        return metric.at[pl.ds(p * shard, shard), pl.ds(0, tile_end(p))]

    def mo_copy(p):
        return remote(metric_ref.at[:, pl.ds(0, tile_end(p))], home_rows(p), mo_send, mo_recv, (b, mate))

    @at_home
    def _(hv, p):
        mo_copy(p).start()

    for p in range(groups):
        @pl.when(p // 2 != h)
        def _():
            for n in range(parts):
                if wide(p, n) < tile_end(p):
                    low = p * shard + 2 * n * part
                    fill = jnp.zeros((2 * part, tile_end(p) - wide(p, n)), metric.dtype)
                    metric[low:low + 2 * part, wide(p, n):tile_end(p)] = fill

    def m1_step(n):
        @away
        def _(hv, p):
            landed(band(p, x, n), m1_recv.at[hv, n])
            m2_copy(hv, p, n).start()
            m3_copy(hv, p, True, n).start()

    def m2_step(n):
        @away
        def _(hv, p):
            landed(band(p, 1 - x, n), m2_recv.at[hv, n])
            m3_copy(hv, p, False, n).start()

    def z_copy(p, k):
        return remote(
            near.at[strip(p, k), first], near.at[strip(p, k), second],
            z_send.at[p, k], ring_recv.at[p, k], (ahead, g),
        )

    def w_copy(p):
        return remote(near.at[rows(p), second], far.at[rows(p)], w_send.at[p], far_recv.at[p], (ahead, mate))

    def sent_up(p):
        return jnp.logical_not((core == x) & (p // 2 == h))

    def f_copy_all(q):
        return remote(fit_a.at[span(q)], fit_b.at[span(q)], f_send.at[q], f_recv.at[q], (b, mate))

    def f_copy_one(q):
        return remote(
            fit_a.at[span(q), second], fit_b.at[span(q), first], f_send.at[q], f_recv.at[q], (b, mate)
        )

    occ_copy.start()
    vir_copy.start()
    vir_copy.wait()
    occ_copy.wait()
    level = jnp.broadcast_to(levels[...], (vir, vir))
    gap[...] = level + level.T

    own_metric.wait()

    @at_home
    def _(hv, p):
        landed(home_rows(p + 1 - 2 * (p % 2)), mo_recv)

    def turn(p):
        @pl.loop(0, p + 1)
        def _(q):
            metric_t[span(q), span(p)] = metric[span(p), span(q)].T

    if tile == shard:
        turn(2 * h)
        turn(2 * h + 1)

    def pass_own(p):
        for k in range(2):
            landed(near.at[strip(p, k), first], h_recv.at[p, k])

            @pl.when(sent_up(p))
            def _():
                z_copy(p, k).start()

    def pass_on(p):
        for k in range(2):
            landed(near.at[strip(p, k), second], ring_recv.at[p, k])

        @pl.when(core == 1)
        def _():
            w_copy(p).start()

    for p in order[:2]:
        pass_own(p)

    @at_home
    def _(hv, p):
        for n in range(parts // 2):
            for r in range(1, pairs):
                m1_copy(hv, p, r, n).start()

    for p in order[2:3]:
        pass_own(p)
    for k in range(2):
        ints_copy(last, k).wait_send()

    @at_home
    def _(hv, p):
        for n in range(parts // 2, parts):
            for r in range(1, pairs):
                m1_copy(hv, p, r, n).start()

    for p in order[3:]:
        pass_own(p)
    for n in range(parts):
        m1_step(n)
        if n >= 2:
            m2_step(n - 2)
    @pl.when(core == 0)
    def _():
        for p in order[:-1]:
            @pl.when(sent_up(p))
            def _():
                for k in range(2):
                    z_copy(p, k).wait_send()
        pl.semaphore_signal(go, inc=1, device_id=(b, mate), device_id_type=MESH)

    @pl.when(core == 1)
    def _():
        pl.semaphore_wait(go, 1)

    pass_on(tail_first[0])
    for n in range(max(parts - 2, 0), parts):
        m2_step(n)
    for p in tail_first[1:]:
        pass_on(p)

    @away
    def _(hv, p):
        other = p + 1 - 2 * (p % 2)
        for n in range(parts):
            landed(band(other, 0, n), m3_recv.at[hv, 0, n])
            landed(band(other, 1, n), m3_recv.at[hv, 1, n])

    if tile == shard:
        for r in range(1, pairs):
            turn(2 * ((h + r) % pairs))
            turn(2 * ((h + r) % pairs) + 1)
    else:
        pl.loop(0, tiles)(turn)

    own_energy = occ[own_b * groups + own_c]

    def amplitude_of(pair, role):
        energy = own_energy + occ[(own_b + blocks - role) % blocks * groups + own_c]
        return ((2.0 * pair.T - pair) / (energy - gap[...])).astype(amp_a.dtype)

    for q in range(tiles):
        low = q * tile
        fit_a[low:low + tile, :] = jnp.dot(
            metric_t[low:low + tile, low:], near[low:, :], preferred_element_type=f32,
        ).astype(fit_a.dtype)

        @pl.when(core == 0)
        def _():
            f_copy_all(q).start()

        @pl.when(core == 1)
        def _():
            f_copy_one(q).start()

        fit_t[:, low:low + tile] = fit_a[low:low + tile, :vir].T

    pair = jnp.dot(fit_t[...], fit_a[...], preferred_element_type=f32)
    amp_a[:vir, :] = amplitude_of(pair[:, :vir], 0)
    amp_a[vir:, :] = amplitude_of(pair[:, vir:], 2)
    dens[...] = jnp.dot(fit_a[...], amp_a[...], preferred_element_type=f32)

    @pl.when(core == 1)
    def _():
        for q in range(tiles):
            landed(fit_b.at[span(q)], f_recv.at[q])
        pair = jnp.dot(fit_t[...], fit_b[...], preferred_element_type=f32)
        amp_b[:vir, :] = amplitude_of(pair[:, :vir], 1)
        amp_b[vir:, :] = amplitude_of(pair[:, vir:], 3)

    @pl.when(core == 0)
    def _():
        for q in range(tiles):
            landed(fit_b.at[span(q), first], f_recv.at[q])
        pair = jnp.dot(fit_t[...], fit_b[:, :vir], preferred_element_type=f32)
        amp_b[:vir, :] = amplitude_of(pair, 1)
        dens[...] += jnp.dot(fit_b[:, :vir], amp_b[:vir, :], preferred_element_type=f32)
        for q in reversed(range(tiles)):
            low = q * tile
            for p in reversed(range(low // shard, (low + tile) // shard)):
                landed(far.at[rows(p)], far_recv.at[p])
            fit_b[low:low + tile, vir:] = jnp.dot(
                metric_t[low:low + tile, low:], far[low:, :], preferred_element_type=f32,
            ).astype(fit_b.dtype)
            part_sum = jnp.dot(
                fit_t[:, low:low + tile], fit_b[low:low + tile, vir:], preferred_element_type=f32
            )
            if q == tiles - 1:
                pair_sum[...] = part_sum
            else:
                pair_sum[...] += part_sum
        amp_b[vir:, :] = amplitude_of(pair_sum[...], 3)

    def g_copy(p):
        return remote(gam.at[rows(p)], out_ref.at[own_c], g_send.at[p], g_recv.at[own_c], (own_b, p))

    def g_self(p):
        return (core == x) & (g == p)

    for t in range(tiles):
        low = t * tile

        @pl.when(core == 0)
        def _():
            total = dens[low:low + tile, :] + jnp.dot(
                fit_b[low:low + tile, vir:], amp_b[vir:, :], preferred_element_type=f32
            )
            dens_b[low:low + tile, :] = total.astype(dens_b.dtype)

        @pl.when(core == 1)
        def _():
            total = dens[low:low + tile, :] + jnp.dot(
                fit_b[low:low + tile, :], amp_b[...], preferred_element_type=f32
            )
            dens_b[low:low + tile, :] = total.astype(dens_b.dtype)

        gam[low:low + tile, :] = jnp.dot(
            metric[low:low + tile, :low + tile], dens_b[:low + tile, :],
            preferred_element_type=f32,
        ).astype(gam.dtype)
        for p in range(low // shard, (low + tile) // shard):
            @pl.when(jnp.logical_not(g_self(p)))
            def _():
                g_copy(p).start()

            @pl.when(g_self(p))
            def _():
                pltpu.make_async_copy(gam.at[rows(p)], out_ref.at[own_c], g_recv.at[own_c]).start()

    for k in range(2):
        d_copy(k).wait_send()

    @pl.when(core == 0)
    def _():
        for p in order[-1:]:
            for k in range(2):
                z_copy(p, k).wait_send()

    for c in range(groups):
        @pl.when(jnp.logical_not(to_self(c)) & (c != last))
        def _():
            for k in range(2):
                ints_copy(c, k).wait_send()

        @pl.when(sent_up(c) & (core == 1))
        def _():
            for k in range(2):
                z_copy(c, k).wait_send()

        @pl.when(core == 1)
        def _():
            w_copy(c).wait_send()

        @pl.when(jnp.logical_not(g_self(c)))
        def _():
            g_copy(c).wait_send()

    for q in range(tiles):
        @pl.when(core == 0)
        def _():
            f_copy_all(q).wait_send()

        @pl.when(core == 1)
        def _():
            f_copy_one(q).wait_send()

    @at_home
    def _(hv, p):
        for n in range(parts):
            for r in range(1, pairs):
                m1_copy(hv, p, r, n).wait_send()
        mo_copy(p).wait_send()

    @away
    def _(hv, p):
        for n in range(parts):
            m2_copy(hv, p, n).wait_send()
            m3_copy(hv, p, True, n).wait_send()
            m3_copy(hv, p, False, n).wait_send()

    for c in range(groups):
        landed(out_ref.at[c], g_recv.at[c])


def hand_over(gam_ref, out_ref, held, in_sem, out_sem):
    units = gam_ref.shape[0]
    for c in range(units):
        pltpu.make_async_copy(gam_ref.at[c], held.at[c], in_sem.at[c]).start()
    for c in range(units):
        pltpu.make_async_copy(gam_ref.at[c], held.at[c], in_sem.at[c]).wait()
        pltpu.make_async_copy(held.at[c], out_ref.at[c], out_sem.at[c]).start()
    for c in range(units):
        pltpu.make_async_copy(held.at[c], out_ref.at[c], out_sem.at[c]).wait()


def local(half_ints, metric_inv, occ_energy, vir_energy):
    groups, blocks = lax.axis_size("aux"), lax.axis_size("blk")
    shard, vir = half_ints.shape[1:]
    naux = metric_inv.shape[1]
    tile = shard if shard % 128 == 0 else naux // 4
    pairs, tiles = groups // 2, naux // tile
    parts = 6 if shard % 192 == 0 else 1
    dma = pltpu.SemaphoreType.DMA
    gamma = pl.pallas_call(
        functools.partial(kernel, blocks, groups, tile),
        out_shape=jax.ShapeDtypeStruct(half_ints.shape, jnp.bfloat16),
        in_specs=[
            pl.BlockSpec(memory_space=pl.ANY),
            pl.BlockSpec(memory_space=pl.ANY),
            pl.BlockSpec(memory_space=pl.ANY),
            pl.BlockSpec(memory_space=pl.ANY),
        ],
        out_specs=pl.BlockSpec(memory_space=pl.ANY),
        scratch_shapes=[
            pltpu.VMEM((naux, 2 * vir), jnp.bfloat16),
            pltpu.VMEM((naux, vir), jnp.bfloat16),
            pltpu.VMEM((naux, naux), jnp.bfloat16),
            pltpu.VMEM((naux, naux), jnp.bfloat16),
            pltpu.VMEM((naux, 2 * vir), jnp.bfloat16),
            pltpu.VMEM((naux, 2 * vir), jnp.bfloat16),
            pltpu.VMEM((vir, naux), jnp.bfloat16),
            pltpu.VMEM((2 * vir, vir), jnp.bfloat16),
            pltpu.VMEM((2 * vir, vir), jnp.bfloat16),
            pltpu.VMEM((vir, vir), jnp.float32),
            pltpu.VMEM((vir, vir), jnp.float32),
            pltpu.VMEM((naux, vir), jnp.float32),
            pltpu.VMEM((naux, vir), jnp.bfloat16),
            pltpu.VMEM((naux, vir), jnp.bfloat16),
            pltpu.SMEM(occ_energy.shape, jnp.float32),
            pltpu.VMEM(vir_energy.shape, jnp.float32),
            dma(()), dma(()), pltpu.SemaphoreType.REGULAR,
            dma((groups, 2)), dma((groups, 2)), dma((2,)), dma((groups, 2)), dma((groups,)), dma((groups, 2)), dma((groups,)),
            dma((tiles,)), dma((tiles,)),
            dma((pairs, parts)), dma((pairs, parts)), dma((pairs, parts)), dma((pairs, parts)),
            dma((pairs, 2, parts)), dma((pairs, 2, parts)), dma(()), dma(()),
            dma(()), dma((groups,)), dma((groups,)),
        ],
        compiler_params=pltpu.CompilerParams(
            collective_id=0, has_side_effects=True, vmem_limit_bytes=56 * 2**20
        ),
    )(half_ints, metric_inv, occ_energy, vir_energy)
    return pl.pallas_call(
        hand_over,
        out_shape=jax.ShapeDtypeStruct(half_ints.shape, jnp.bfloat16),
        in_specs=[pl.BlockSpec(memory_space=pl.ANY)],
        out_specs=pl.BlockSpec(memory_space=pl.ANY),
        scratch_shapes=[pltpu.VMEM(half_ints.shape, jnp.bfloat16), dma((groups,)), dma((groups,))],
    )(gamma)


def solution(mesh):
    placed = (P("blk", "aux", None), P("aux", None), P(), P())
    return jax.shard_map(
        local, mesh=mesh, in_specs=placed, out_specs=P("blk", "aux", None), check_vma=False
    )
```

```python
import functools

import jax
import jax.numpy as jnp
from jax import lax
from jax.experimental import pallas as pl
from jax.experimental.pallas import tpu as pltpu
from jax.sharding import PartitionSpec as P

MESH = pl.DeviceIdType.MESH


def kernel(
    blocks, groups, tile,
    ints_ref, metric_ref, occ_ref, vir_ref,
    out_ref,
    near, far, metric, metric_t, fit_a, fit_b, fit_t, amp_a, amp_b, gap, pair_sum, carry, dens, dens_b, gam, occ, levels,
    occ_sem, vir_sem, go, h_send, h_recv, d_send, z_send, w_send, ring_recv, far_recv, f_send, f_recv,
    m1_send, m1_recv, m2_send, m2_recv, m3_send, m3_recv, mo_send, mo_recv, own_sem, g_send, g_recv,
):
    shard = ints_ref.shape[1]
    half = shard // 2
    parts = 6 if half % 96 == 0 else 1
    part = half // parts
    naux = metric_ref.shape[1]
    vir = ints_ref.shape[2]
    tiles = naux // tile
    pairs = groups // 2
    b, g = lax.axis_index("blk"), lax.axis_index("aux")
    x, core, h = b % 2, g % 2, g // 2
    plane, mate, ahead = b - x, g + 1 - 2 * core, (b + 2) % blocks
    across = b + 1 - 2 * x
    own_b, own_c = plane + core, g - core + x
    f32 = jnp.float32

    def rows(p):
        return pl.ds(pl.multiple_of(p * shard, shard), shard)

    def span(q):
        return pl.ds(pl.multiple_of(q * tile, tile), tile)

    def wide(p, n):
        return min(naux, -(-(p * shard + 2 * (n + 1) * part) // 128) * 128)

    def tile_end(p):
        return (p * shard // tile + 1) * tile

    def remote(src, dst, send, recv, device):
        return pltpu.make_async_remote_copy(
            src_ref=src, dst_ref=dst, send_sem=send, recv_sem=recv,
            device_id=device, device_id_type=MESH,
        )

    def landed(dst, recv):
        pltpu.make_async_copy(dst, dst, recv).wait()

    first, second = pl.ds(0, vir), pl.ds(vir, vir)
    occ_copy = pltpu.make_async_copy(occ_ref, occ, occ_sem)
    vir_copy = pltpu.make_async_copy(vir_ref, levels, vir_sem)
    barrier = pltpu.get_barrier_semaphore()
    for xx in range(2):
        for gg in range(groups):
            @pl.when((plane + xx != b) | (gg != g))
            def _():
                pl.semaphore_signal(barrier, inc=1, device_id=(plane + xx, gg), device_id_type=MESH)
    for bb in (ahead, (b + blocks - 2) % blocks):
        for gg in (g, mate):
            pl.semaphore_signal(barrier, inc=1, device_id=(bb, gg), device_id_type=MESH)
    pl.semaphore_wait(barrier, 2 * groups + 3)

    def strip(p, k):
        return pl.ds(pl.multiple_of(p * shard + k * half, half), half)

    def ints_copy(c, k):
        return remote(
            ints_ref.at[c, pl.ds(k * half, half)], near.at[strip(g, k), first],
            h_send.at[c, k], h_recv.at[g, k], (plane + c % 2, c - c % 2 + x),
        )

    def to_self(c):
        return (core == x) & (c == own_c)

    order = [(2 * ((h + r) % pairs) + par) for r in range(pairs) for par in range(2)]
    last = 2 * ((h + pairs - 1) % pairs) + 1 - x
    tail_first = [groups - 2] + [p for p in range(groups - 1, -1, -1) if p != groups - 2]

    def d_copy(k):
        return remote(
            ints_ref.at[own_c, pl.ds(k * half, half)], near.at[strip(g, k), second],
            d_send.at[k], ring_recv.at[g, k], (ahead, own_c),
        )

    for k in range(2):
        d_copy(k).start()
    for c in order:
        @pl.when(jnp.logical_not(to_self(c)))
        def _():
            for k in range(2):
                ints_copy(c, k).start()

        @pl.when(to_self(c))
        def _():
            for k in range(2):
                pltpu.make_async_copy(
                    ints_ref.at[c, pl.ds(k * half, half)], near.at[strip(g, k), first], h_recv.at[g, k]
                ).start()

    own_metric = pltpu.make_async_copy(metric_ref, metric.at[rows(g)], own_sem)
    own_metric.start()

    def at_home(act):
        for hv in range(pairs):
            for cc in range(2):
                @pl.when((h == hv) & (core == cc))
                def _():
                    act(hv, 2 * hv + cc)

    def away(act):
        for hv in range(pairs):
            for cc in range(2):
                @pl.when((h != hv) & (core == cc))
                def _():
                    act(hv, 2 * hv + cc)

    def band(p, which, n):
        low = pl.multiple_of(p * shard + (2 * n + which) * part, part)
        return metric.at[pl.ds(low, part), pl.ds(0, wide(p, n))]

    def m1_copy(hv, p, r, n):
        low = pl.multiple_of((2 * n + x) * part, part)
        return remote(
            metric_ref.at[pl.ds(low, part), pl.ds(0, wide(p, n))], band(p, x, n),
            m1_send.at[r, n], m1_recv.at[hv, n], (b, 2 * ((h + r) % pairs) + core),
        )

    def m2_copy(hv, p, n):
        return remote(band(p, x, n), band(p, x, n), m2_send.at[hv, n], m2_recv.at[hv, n], (across, g))

    def m3_copy(hv, p, own, n):
        which = x if own else 1 - x
        return remote(
            band(p, which, n), band(p, which, n),
            m3_send.at[hv, which, n], m3_recv.at[hv, which, n], (b, mate),
        )

    def home_rows(p):
        return metric.at[pl.ds(p * shard, shard), pl.ds(0, tile_end(p))]

    def mo_copy(p):
        return remote(metric_ref.at[:, pl.ds(0, tile_end(p))], home_rows(p), mo_send, mo_recv, (b, mate))

    @at_home
    def _(hv, p):
        mo_copy(p).start()

    for p in range(groups):
        @pl.when(p // 2 != h)
        def _():
            for n in range(parts):
                if wide(p, n) < tile_end(p):
                    low = p * shard + 2 * n * part
                    fill = jnp.zeros((2 * part, tile_end(p) - wide(p, n)), metric.dtype)
                    metric[low:low + 2 * part, wide(p, n):tile_end(p)] = fill

    def m1_step(n):
        @away
        def _(hv, p):
            landed(band(p, x, n), m1_recv.at[hv, n])
            m2_copy(hv, p, n).start()
            m3_copy(hv, p, True, n).start()

    def m2_step(n):
        @away
        def _(hv, p):
            landed(band(p, 1 - x, n), m2_recv.at[hv, n])
            m3_copy(hv, p, False, n).start()

    def z_copy(p, k):
        return remote(
            near.at[strip(p, k), first], near.at[strip(p, k), second],
            z_send.at[p, k], ring_recv.at[p, k], (ahead, g),
        )

    def w_copy(p):
        return remote(near.at[rows(p), second], far.at[rows(p)], w_send.at[p], far_recv.at[p], (ahead, mate))

    def sent_up(p):
        return jnp.logical_not((core == x) & (p // 2 == h))

    def f_copy_all(q):
        return remote(fit_a.at[span(q)], fit_b.at[span(q)], f_send.at[q], f_recv.at[q], (b, mate))

    def f_copy_one(q):
        return remote(
            fit_a.at[span(q), second], fit_b.at[span(q), first], f_send.at[q], f_recv.at[q], (b, mate)
        )

    occ_copy.start()
    vir_copy.start()
    vir_copy.wait()
    occ_copy.wait()
    level = jnp.broadcast_to(levels[...], (vir, vir))
    gap[...] = level + level.T

    own_metric.wait()

    @at_home
    def _(hv, p):
        landed(home_rows(p + 1 - 2 * (p % 2)), mo_recv)

    def turn(p):
        @pl.loop(0, p + 1)
        def _(q):
            metric_t[span(q), span(p)] = metric[span(p), span(q)].T

    if tile == shard:
        turn(2 * h)
        turn(2 * h + 1)

    def pass_own(p):
        for k in range(2):
            landed(near.at[strip(p, k), first], h_recv.at[p, k])

            @pl.when(sent_up(p))
            def _():
                z_copy(p, k).start()

    def pass_on(p):
        for k in range(2):
            landed(near.at[strip(p, k), second], ring_recv.at[p, k])

        @pl.when(core == 1)
        def _():
            w_copy(p).start()

    for p in order[:2]:
        pass_own(p)

    @at_home
    def _(hv, p):
        for n in range(parts // 2):
            for r in range(1, pairs):
                m1_copy(hv, p, r, n).start()

    for p in order[2:3]:
        pass_own(p)
    for k in range(2):
        ints_copy(last, k).wait_send()

    @at_home
    def _(hv, p):
        for n in range(parts // 2, parts):
            for r in range(1, pairs):
                m1_copy(hv, p, r, n).start()

    for p in order[3:]:
        pass_own(p)
    for n in range(parts):
        m1_step(n)
        if n >= 2:
            m2_step(n - 2)
    @pl.when(core == 0)
    def _():
        for p in order[:-1]:
            @pl.when(sent_up(p))
            def _():
                for k in range(2):
                    z_copy(p, k).wait_send()
        pl.semaphore_signal(go, inc=1, device_id=(b, mate), device_id_type=MESH)

    @pl.when(core == 1)
    def _():
        pl.semaphore_wait(go, 1)

    pass_on(tail_first[0])
    for n in range(max(parts - 2, 0), parts):
        m2_step(n)
    for p in tail_first[1:]:
        pass_on(p)

    @away
    def _(hv, p):
        other = p + 1 - 2 * (p % 2)
        for n in range(parts):
            landed(band(other, 0, n), m3_recv.at[hv, 0, n])
            landed(band(other, 1, n), m3_recv.at[hv, 1, n])

    if tile == shard:
        for r in range(1, pairs):
            turn(2 * ((h + r) % pairs))
            turn(2 * ((h + r) % pairs) + 1)
    else:
        pl.loop(0, tiles)(turn)

    own_energy = occ[own_b * groups + own_c]

    def amplitude_of(pair, role):
        energy = own_energy + occ[(own_b + blocks - role) % blocks * groups + own_c]
        return ((2.0 * pair.T - pair) / (energy - gap[...])).astype(amp_a.dtype)

    for q in range(tiles):
        low = q * tile
        fit_a[low:low + tile, :] = jnp.dot(
            metric_t[low:low + tile, low:], near[low:, :], preferred_element_type=f32,
        ).astype(fit_a.dtype)

        @pl.when(core == 0)
        def _():
            f_copy_all(q).start()

        @pl.when(core == 1)
        def _():
            f_copy_one(q).start()

        fit_t[:, low:low + tile] = fit_a[low:low + tile, :vir].T

    pair = jnp.dot(fit_t[...], fit_a[...], preferred_element_type=f32)
    amp_a[:vir, :] = amplitude_of(pair[:, :vir], 0)
    amp_a[vir:, :] = amplitude_of(pair[:, vir:], 2)
    dens[...] = jnp.dot(fit_a[...], amp_a[...], preferred_element_type=f32)

    @pl.when(core == 1)
    def _():
        for q in range(tiles):
            landed(fit_b.at[span(q)], f_recv.at[q])
        pair = jnp.dot(fit_t[...], fit_b[...], preferred_element_type=f32)
        amp_b[:vir, :] = amplitude_of(pair[:, :vir], 1)
        amp_b[vir:, :] = amplitude_of(pair[:, vir:], 3)

    @pl.when(core == 0)
    def _():
        for q in range(tiles):
            landed(fit_b.at[span(q), first], f_recv.at[q])
        pair = jnp.dot(fit_t[...], fit_b[:, :vir], preferred_element_type=f32)
        amp_b[:vir, :] = amplitude_of(pair, 1)
        dens[...] += jnp.dot(fit_b[:, :vir], amp_b[:vir, :], preferred_element_type=f32)
        for q in reversed(range(tiles)):
            low = q * tile
            if q < tiles - 1:
                carry[...] = jnp.dot(
                    metric_t[low:low + tile, low + tile:], far[low + tile:, :], preferred_element_type=f32
                )
            for p in reversed(range(low // shard, (low + tile) // shard)):
                landed(far.at[rows(p)], far_recv.at[p])
            block = jnp.dot(
                metric_t[low:low + tile, low:low + tile], far[low:low + tile, :], preferred_element_type=f32
            )
            if q < tiles - 1:
                block += carry[...]
            fit_b[low:low + tile, vir:] = block.astype(fit_b.dtype)
            part_sum = jnp.dot(
                fit_t[:, low:low + tile], fit_b[low:low + tile, vir:], preferred_element_type=f32
            )
            if q == tiles - 1:
                pair_sum[...] = part_sum
            else:
                pair_sum[...] += part_sum
        amp_b[vir:, :] = amplitude_of(pair_sum[...], 3)

    def g_copy(p):
        return remote(gam.at[rows(p)], out_ref.at[own_c], g_send.at[p], g_recv.at[own_c], (own_b, p))

    def g_self(p):
        return (core == x) & (g == p)

    for t in range(tiles):
        low = t * tile

        @pl.when(core == 0)
        def _():
            total = dens[low:low + tile, :] + jnp.dot(
                fit_b[low:low + tile, vir:], amp_b[vir:, :], preferred_element_type=f32
            )
            dens_b[low:low + tile, :] = total.astype(dens_b.dtype)

        @pl.when(core == 1)
        def _():
            total = dens[low:low + tile, :] + jnp.dot(
                fit_b[low:low + tile, :], amp_b[...], preferred_element_type=f32
            )
            dens_b[low:low + tile, :] = total.astype(dens_b.dtype)

        gam[low:low + tile, :] = jnp.dot(
            metric[low:low + tile, :low + tile], dens_b[:low + tile, :],
            preferred_element_type=f32,
        ).astype(gam.dtype)
        for p in range(low // shard, (low + tile) // shard):
            @pl.when(jnp.logical_not(g_self(p)))
            def _():
                g_copy(p).start()

            @pl.when(g_self(p))
            def _():
                pltpu.make_async_copy(gam.at[rows(p)], out_ref.at[own_c], g_recv.at[own_c]).start()

    for k in range(2):
        d_copy(k).wait_send()

    @pl.when(core == 0)
    def _():
        for p in order[-1:]:
            for k in range(2):
                z_copy(p, k).wait_send()

    for c in range(groups):
        @pl.when(jnp.logical_not(to_self(c)) & (c != last))
        def _():
            for k in range(2):
                ints_copy(c, k).wait_send()

        @pl.when(sent_up(c) & (core == 1))
        def _():
            for k in range(2):
                z_copy(c, k).wait_send()

        @pl.when(core == 1)
        def _():
            w_copy(c).wait_send()

        @pl.when(jnp.logical_not(g_self(c)))
        def _():
            g_copy(c).wait_send()

    for q in range(tiles):
        @pl.when(core == 0)
        def _():
            f_copy_all(q).wait_send()

        @pl.when(core == 1)
        def _():
            f_copy_one(q).wait_send()

    @at_home
    def _(hv, p):
        for n in range(parts):
            for r in range(1, pairs):
                m1_copy(hv, p, r, n).wait_send()
        mo_copy(p).wait_send()

    @away
    def _(hv, p):
        for n in range(parts):
            m2_copy(hv, p, n).wait_send()
            m3_copy(hv, p, True, n).wait_send()
            m3_copy(hv, p, False, n).wait_send()

    for c in range(groups):
        landed(out_ref.at[c], g_recv.at[c])


def hand_over(gam_ref, out_ref, held, in_sem, out_sem):
    units = gam_ref.shape[0]
    for c in range(units):
        pltpu.make_async_copy(gam_ref.at[c], held.at[c], in_sem.at[c]).start()
    for c in range(units):
        pltpu.make_async_copy(gam_ref.at[c], held.at[c], in_sem.at[c]).wait()
        pltpu.make_async_copy(held.at[c], out_ref.at[c], out_sem.at[c]).start()
    for c in range(units):
        pltpu.make_async_copy(held.at[c], out_ref.at[c], out_sem.at[c]).wait()


def local(half_ints, metric_inv, occ_energy, vir_energy):
    groups, blocks = lax.axis_size("aux"), lax.axis_size("blk")
    shard, vir = half_ints.shape[1:]
    naux = metric_inv.shape[1]
    tile = shard if shard % 128 == 0 else naux // 4
    pairs, tiles = groups // 2, naux // tile
    parts = 6 if shard % 192 == 0 else 1
    dma = pltpu.SemaphoreType.DMA
    gamma = pl.pallas_call(
        functools.partial(kernel, blocks, groups, tile),
        out_shape=jax.ShapeDtypeStruct(half_ints.shape, jnp.bfloat16),
        in_specs=[
            pl.BlockSpec(memory_space=pl.ANY),
            pl.BlockSpec(memory_space=pl.ANY),
            pl.BlockSpec(memory_space=pl.ANY),
            pl.BlockSpec(memory_space=pl.ANY),
        ],
        out_specs=pl.BlockSpec(memory_space=pl.ANY),
        scratch_shapes=[
            pltpu.VMEM((naux, 2 * vir), jnp.bfloat16),
            pltpu.VMEM((naux, vir), jnp.bfloat16),
            pltpu.VMEM((naux, naux), jnp.bfloat16),
            pltpu.VMEM((naux, naux), jnp.bfloat16),
            pltpu.VMEM((naux, 2 * vir), jnp.bfloat16),
            pltpu.VMEM((naux, 2 * vir), jnp.bfloat16),
            pltpu.VMEM((vir, naux), jnp.bfloat16),
            pltpu.VMEM((2 * vir, vir), jnp.bfloat16),
            pltpu.VMEM((2 * vir, vir), jnp.bfloat16),
            pltpu.VMEM((vir, vir), jnp.float32),
            pltpu.VMEM((vir, vir), jnp.float32),
            pltpu.VMEM((tile, vir), jnp.float32),
            pltpu.VMEM((naux, vir), jnp.float32),
            pltpu.VMEM((naux, vir), jnp.bfloat16),
            pltpu.VMEM((naux, vir), jnp.bfloat16),
            pltpu.SMEM(occ_energy.shape, jnp.float32),
            pltpu.VMEM(vir_energy.shape, jnp.float32),
            dma(()), dma(()), pltpu.SemaphoreType.REGULAR,
            dma((groups, 2)), dma((groups, 2)), dma((2,)), dma((groups, 2)), dma((groups,)), dma((groups, 2)), dma((groups,)),
            dma((tiles,)), dma((tiles,)),
            dma((pairs, parts)), dma((pairs, parts)), dma((pairs, parts)), dma((pairs, parts)),
            dma((pairs, 2, parts)), dma((pairs, 2, parts)), dma(()), dma(()),
            dma(()), dma((groups,)), dma((groups,)),
        ],
        compiler_params=pltpu.CompilerParams(
            collective_id=0, has_side_effects=True, vmem_limit_bytes=56 * 2**20
        ),
    )(half_ints, metric_inv, occ_energy, vir_energy)
    return pl.pallas_call(
        hand_over,
        out_shape=jax.ShapeDtypeStruct(half_ints.shape, jnp.bfloat16),
        in_specs=[pl.BlockSpec(memory_space=pl.ANY)],
        out_specs=pl.BlockSpec(memory_space=pl.ANY),
        scratch_shapes=[pltpu.VMEM(half_ints.shape, jnp.bfloat16), dma((groups,)), dma((groups,))],
    )(gamma)


def solution(mesh):
    placed = (P("blk", "aux", None), P("aux", None), P(), P())
    return jax.shard_map(
        local, mesh=mesh, in_specs=placed, out_specs=P("blk", "aux", None), check_vma=False
    )
```
